32 devices in a mesh: seq: 4 (over x, core), mp: 8 (over z, y).
Axes of the slice: x: 2, y: 2, z: 4, core: 2. Of those that a mesh axis runs over, the one named last changes fastest.
Arguments:
- signal: bfloat16 [2048, 8192], P('seq', 'mp'), may hold values from -6 to 6
- gate_input: bfloat16 [2048, 8192], P('seq', 'mp'), may hold values from -6 to 6
- input_map: bfloat16 [2048, 128], P('seq'), may hold values from -0.5 to 0.5
- output_map: bfloat16 [2048, 128], P('seq'), may hold values from -6 to 6
- log_decay: float32 [2048, 128], P('seq', 'mp'), may hold values from -1 to 0
- step_size: float32 [2048, 128], P('seq', 'mp'), may hold values from 0.003 to 0.03
- skip_gain: float32 [128], P('mp'), may hold values from 0.1 to 1.9
- norm_gain: float32 [8192], P('mp'), may hold values from 0.1 to 1.9
- out_weight: bfloat16 [8192, 8192], P('mp'), may hold values from -0.09375 to 0.09375
Outputs:
- mixed_out: bfloat16 [2048, 8192], P('seq', 'mp')
The draws below stay inside these ranges and needn't reach their ends.
All inputs are finite; a program needn't handle non-finite values.
Results may differ from the reference program's by a relative error of at most 0.024.
Values may be sent and summed in bfloat16 or wider, within the bound.
A program may use at most 64 MiB of HBM per device.

```python
import math
import jax
import jax.numpy as jnp
from jax import lax

D = 8192
HEADS = 128
HEAD_DIM = 64
STATE = 128
BLOCK = 256
TOK_DEV = 512
INNER = 8192
TOKEN_COUNT = 2048
N_MP = 8


def draw_log_decay(key, part):
    subkeys = jax.random.split(key, 7)
    fast_share = 0.4
    fast_heads = jax.random.uniform(subkeys[0], (HEADS,)) < fast_share
    fast_rates = jnp.exp(jax.random.uniform(subkeys[1], (HEADS,), minval=math.log(1.0 / 50.0), maxval=math.log(1.0 / 30.0)))
    slow_rates = jnp.exp(jax.random.uniform(subkeys[2], (HEADS,), minval=math.log(0.02), maxval=math.log(0.25))) * 2.3 / TOKEN_COUNT
    baseline_rates = jnp.where(fast_heads, fast_rates, slow_rates)
    surface_rough = jnp.exp(jax.random.uniform(subkeys[3], (TOKEN_COUNT, HEADS), minval=-math.log(2.0), maxval=math.log(2.0)))
    processor_factor = jnp.exp(jax.random.uniform(subkeys[4], (TOKEN_COUNT // TOK_DEV, 1), minval=-math.log(2.0), maxval=math.log(2.0)))
    processor_factor = jnp.repeat(processor_factor, TOK_DEV, axis=0)
    token_positions = jax.random.randint(subkeys[5], (2,), 0, TOKEN_COUNT)
    spike_row_set = jnp.any(jnp.arange(TOKEN_COUNT)[:, None] == token_positions[None, :], axis=1)
    loss_values = jnp.log(jax.random.uniform(subkeys[6], (TOKEN_COUNT, HEADS), minval=0.5, maxval=0.8))
    value_entries = -(baseline_rates[None, :] * surface_rough * processor_factor) + jnp.where(spike_row_set[:, None], loss_values, 0.0)
    return value_entries.astype(jnp.float32)


def raised(values, key, source, target, shards_of, factor):
    owner, partner = [(jnp.arange(values.shape[dim]) // (values.shape[dim] // shards_of)).reshape([-1 if axis == dim else 1 for axis in range(values.ndim)]) for dim in (source, target)]
    chosen = jax.random.permutation(key, shards_of)[partner]
    strong = (owner == chosen) | (owner == (partner + shards_of // 2) % shards_of)
    return jnp.where(strong, factor * values, values)


def steps_of(key, dims, cuts, low, top_value):
    def one(position, blocks):
        heights = jax.random.uniform(jax.random.fold_in(jax.random.fold_in(key, 6), position), (blocks,), jnp.float32, low / len(cuts), top_value / len(cuts))
        return jnp.repeat(jnp.exp(heights), dims[position] // blocks).reshape((-1,) + (1,) * (len(dims) - position - 1))

    level = one(*cuts[0])
    for cut in cuts[1:]:
        level = level * one(*cut)
    return level


def gaussian(own_key, shape, spread, reach, cuts=(), held_as=jnp.bfloat16):
    values = jax.random.normal(own_key, shape, jnp.float32) * spread
    if len(cuts) > 0:
        values = steps_of(own_key, shape, cuts, -0.22, 0.18) * values
    return jnp.clip(values, min=-reach, max=reach).astype(held_as)


def noise_with(own_key, extent, scale, most, shards, heavy, dtype=jnp.bfloat16):
    drawn = scale * jax.random.normal(own_key, extent, jnp.float32)
    if shards:
        drawn = drawn * steps_of(own_key, extent, shards, -0.22, 0.18)
    return jnp.clip(raised(drawn, jax.random.fold_in(own_key, 3), *heavy), -most, most).astype(dtype)


def setup_inputs(seed: int = 0) -> dict:
    streams_of = jax.random.split(jax.random.key(seed), 10)
    signal = gaussian(streams_of[0], (TOKEN_COUNT, INNER), 1.0, 6.0, ((0, 4), (1, 8)))
    gate_input = gaussian(streams_of[1], (TOKEN_COUNT, INNER), 1.0, 6.0, ((0, 4), (1, 8)))
    input_map = gaussian(streams_of[2], (TOKEN_COUNT, STATE), STATE ** -0.5, 0.5, ((0, 4),))
    output_map = gaussian(streams_of[3], (TOKEN_COUNT, STATE), 1.0, 6.0, ((0, 4),))
    log_decay = draw_log_decay(jax.random.fold_in(streams_of[9], 71), 0)
    step_size = jnp.clip(jnp.exp(math.log(0.03) - 2.3025851 * jax.random.uniform(streams_of[5], (TOKEN_COUNT, HEADS), jnp.float32) ** steps_of(streams_of[5], (TOKEN_COUNT, HEADS), ((0, 4), (1, 8)), -0.2, 0.2)), 0.003, 0.03)
    skip_gain = jnp.clip(1.0 + 0.18 * jax.random.normal(streams_of[6], (HEADS,), jnp.float32), 0.1, 1.9)
    norm_gain = jnp.clip(1.0 + 0.18 * jax.random.normal(streams_of[7], (INNER,), jnp.float32), 0.1, 1.9)
    out_weight = noise_with(streams_of[8], (INNER, D), INNER ** -0.5, 0.09375, ((0, 8),), (0, 1, 8, 2.0))
    return dict(signal=signal, gate_input=gate_input, input_map=input_map, output_map=output_map, log_decay=log_decay, step_size=step_size, skip_gain=skip_gain, norm_gain=norm_gain, out_weight=out_weight)


def block_terms(pieces):
    signal_blk, keys_blk, query_blk, decay_blk, steps_blk = pieces
    cumulative = jnp.cumsum(decay_blk, axis=0)
    scores = jnp.dot(query_blk, keys_blk.T, preferred_element_type=jnp.float32)
    log_gaps = cumulative[:, None, :] - cumulative[None, :, :]
    causal = jnp.arange(BLOCK)[:, None] >= jnp.arange(BLOCK)[None, :]
    decays = jnp.exp(jnp.where(causal[:, :, None], log_gaps, -jnp.inf))
    weights = (scores[:, :, None] * decays * steps_blk[None, :, :]).astype(jnp.bfloat16)
    inner_part = jnp.einsum('tsh,shp->thp', weights.astype(jnp.float32), signal_blk.astype(jnp.float32))
    feed_rows = (signal_blk.astype(jnp.float32) * (steps_blk * jnp.exp(cumulative[-1] - cumulative))[:, :, None]).astype(jnp.bfloat16)
    local_state = jnp.einsum('shp,sn->hpn', feed_rows.astype(jnp.float32), keys_blk.astype(jnp.float32))
    return (inner_part, local_state, cumulative)

def reference(signal, gate_input, input_map, output_map, log_decay, step_size, skip_gain, norm_gain, out_weight):
    block_count = TOKEN_COUNT // BLOCK
    signal_blk = signal.reshape(block_count, BLOCK, HEADS, HEAD_DIM)
    keys_blk = input_map.reshape(block_count, BLOCK, STATE)
    query_blk = output_map.reshape(block_count, BLOCK, STATE)
    decay_blk = log_decay.reshape(block_count, BLOCK, HEADS)
    steps_blk = step_size.reshape(block_count, BLOCK, HEADS)
    inner_part, local_state, cumulative = lax.map(block_terms, (signal_blk, keys_blk, query_blk, decay_blk, steps_blk))
    block_total = cumulative[:, -1, :]

    def advance(running, pieces):
        total_here, local_here = pieces
        return (jnp.exp(total_here)[:, None, None] * running + local_here, running)
    start_state = jnp.zeros((HEADS, HEAD_DIM, STATE), jnp.float32)
    unused_end, carried = lax.scan(advance, start_state, (block_total, local_state))
    carried_bf = carried.astype(jnp.bfloat16)
    inter = jnp.exp(cumulative)[..., None] * jnp.einsum('btn,bhpn->bthp', query_blk.astype(jnp.float32), carried_bf.astype(jnp.float32))
    ssd_out = inner_part + inter + skip_gain[None, None, :, None] * signal_blk.astype(jnp.float32)
    ssd_out = ssd_out.reshape(TOKEN_COUNT, INNER)
    gated_out = ssd_out * jax.nn.silu(gate_input.astype(jnp.float32))
    squares = lax.optimization_barrier(jnp.sum(gated_out * gated_out, axis=1))
    scaling = 1.0 / jnp.sqrt(squares / INNER + 1e-05)
    gained = (gated_out * norm_gain[None, :]).astype(jnp.bfloat16)
    group_width = INNER // N_MP
    summed = jnp.zeros((TOKEN_COUNT, D), jnp.float32)
    for group_number in range(N_MP):
        lower = group_number * group_width
        partial_value = jnp.dot(gained[:, lower:lower + group_width], out_weight[lower:lower + group_width], preferred_element_type=jnp.float32).astype(jnp.bfloat16)
        partial_value = lax.optimization_barrier(partial_value)
        summed = summed + partial_value.astype(jnp.float32)
    return (scaling[:, None] * summed).astype(jnp.bfloat16)
```

```python
import jax
import jax.numpy as jnp
from jax import lax
from jax.experimental import pallas as pl
from jax.experimental.pallas import tpu as pltpu
from jax.sharding import PartitionSpec as P

BLOCK = 256
MESH = pl.DeviceIdType.MESH


def from_behind(value, axis, steps):
    count = lax.axis_size(axis)
    leading, last = (max(0, -steps), min(count, count - steps))
    return lax.ppermute(value, axis, [(source, source + steps) for source in range(leading, last)])


def on_device(
    signal,
    gate_input,
    input_map,
    output_map,
    log_decay,
    step_size,
    skip_gain,
    norm_gain,
    out_weight,
):
    local_tokens = signal.shape[0]
    inner_width = signal.shape[1]
    heads_here = log_decay.shape[1]
    head_width = inner_width // heads_here
    state_width = input_map.shape[1]
    block_count = local_tokens // BLOCK
    signal_blk = signal.reshape(block_count, BLOCK, heads_here, head_width)
    keys_blk = input_map.reshape(block_count, BLOCK, state_width)
    query_blk = output_map.reshape(block_count, BLOCK, state_width)
    decay_blk = log_decay.reshape(block_count, BLOCK, heads_here)
    steps_blk = step_size.reshape(block_count, BLOCK, heads_here)
    cumulative = jnp.cumsum(decay_blk, axis=1)
    scores = jnp.einsum("btn,bsn->bts", query_blk, keys_blk, preferred_element_type=jnp.float32)
    cum_heads = jnp.swapaxes(cumulative, 1, 2)
    log_gaps = cum_heads[:, :, :, None] - cum_heads[:, :, None, :]
    causal = jnp.arange(BLOCK)[:, None] >= jnp.arange(BLOCK)[None, :]
    decays = jnp.exp(jnp.where(causal, log_gaps, -jnp.inf))
    weights = (scores[:, None] * decays * jnp.swapaxes(steps_blk, 1, 2)[:, :, None, :]).astype(
        jnp.bfloat16
    )
    inner_part = jnp.einsum(
        "bhts,bshp->bthp", weights, signal_blk, preferred_element_type=jnp.float32
    )
    feed_rows = (
        signal_blk * (steps_blk * jnp.exp(cumulative[:, -1:, :] - cumulative))[..., None]
    ).astype(jnp.bfloat16)
    local_state = jnp.einsum(
        "bshp,bsn->bhpn", feed_rows, keys_blk, preferred_element_type=jnp.float32
    )
    block_total = cumulative[:, -1, :]
    dev_total = jnp.sum(block_total, axis=0)
    running = jnp.zeros((heads_here, head_width, state_width), jnp.float32)
    for number in range(block_count):
        running = jnp.exp(block_total[number])[:, None, None] * running + local_state[number]
    dev_state = running

    def relay_step(number, incoming):
        outgoing = jnp.exp(dev_total)[:, None, None] * incoming + dev_state
        return from_behind(outgoing.astype(jnp.bfloat16), "seq", 1).astype(outgoing.dtype)

    incoming = lax.fori_loop(0, lax.axis_size("seq") - 1, relay_step, jnp.zeros_like(dev_state))
    running = incoming
    carried = []
    for number in range(block_count):
        carried.append(running)
        running = jnp.exp(block_total[number])[:, None, None] * running + local_state[number]
    carried_bf = jnp.stack(carried).astype(jnp.bfloat16)
    inter = jnp.exp(cumulative)[..., None] * jnp.einsum(
        "btn,bhpn->bthp", query_blk, carried_bf, preferred_element_type=jnp.float32
    )
    ssd_out = inner_part + inter + skip_gain[None, None, :, None] * signal_blk
    ssd_out = ssd_out.reshape(local_tokens, inner_width)
    gated_out = ssd_out * jax.nn.silu(gate_input.astype(jnp.float32))
    squares = jnp.sum(gated_out * gated_out, axis=1)
    gained = (gated_out * norm_gain[None, :]).astype(jnp.bfloat16)
    return project(gained, jnp.broadcast_to(squares[None], (8, local_tokens)), out_weight)


PAIRS = 2
CHUNKS = 4


def step_target(step, zm, lines):
    up = zm // (lines // 2)
    near = zm * (1 - up) + (lines - 1 - zm) * up
    if step == lines - 1:
        return zm
    turned = (step + near) // (lines - 1)
    seen = (lines - 1 - step) * (1 - turned) + (step - (lines - 1 - near)) * turned
    return seen * (1 - up) + (lines - 1 - seen) * up


def project_kernel(
    gained_ref,
    squares_ref,
    weight_ref,
    out_ref,
    wbuf,
    peer_out,
    peer_in,
    own,
    from_low,
    from_high,
    total,
    sq_in,
    w_sem,
    y_send,
    y_recv,
    z_send,
    low_recv,
    high_recv,
    sq_send,
    sq_recv,
):
    me = lax.axis_index("mp")
    lines = own.shape[0]
    count = lines * PAIRS
    zm = me // PAIRS
    ym = me % PAIRS
    tokens = gained_ref.shape[0]
    width = out_ref.shape[1]
    rows = tokens // CHUNKS
    tile = min(256, width)

    barrier = pltpu.get_barrier_semaphore()
    for d in range(1, count):
        pl.semaphore_signal(
            barrier, inc=1, device_id={"mp": (me + d) % count}, device_id_type=MESH
        )

    targets = [step_target(s, zm, lines) for s in range(lines)]
    columns = [z * PAIRS + 1 - ym for z in targets] + [z * PAIRS + ym for z in targets]

    def w_copy(t):
        cols = pl.ds(pl.multiple_of(columns[t] * width, width), width)
        return pltpu.make_async_copy(weight_ref.at[:, cols], wbuf.at[t], w_sem.at[t])

    for t in range(2 * lines):
        w_copy(t).start()

    def multiply(t, dest, slot):
        w_copy(t).wait()

        @pl.loop(0, width // tile)
        def _(i):
            cols = pl.ds(pl.multiple_of(i * tile, tile), tile)
            dest[slot, :, cols] = jnp.dot(
                gained_ref[...], wbuf[t, :, cols], preferred_element_type=jnp.float32
            ).astype(jnp.bfloat16)

    def y_copy(s, c):
        part = pl.ds(c * rows, rows)
        return pltpu.make_async_remote_copy(
            src_ref=peer_out.at[s, part],
            dst_ref=peer_in.at[s, part],
            send_sem=y_send.at[s, c],
            recv_sem=y_recv.at[s, c],
            device_id={"mp": zm * PAIRS + 1 - ym},
            device_id_type=MESH,
        )

    def sq_copy(d):
        return pltpu.make_async_remote_copy(
            src_ref=squares_ref,
            dst_ref=sq_in.at[me],
            send_sem=sq_send.at[d],
            recv_sem=sq_recv.at[me],
            device_id={"mp": (me + d) % count},
            device_id_type=MESH,
        )

    def sq_arrival(source):
        return pltpu.make_async_remote_copy(
            src_ref=squares_ref,
            dst_ref=sq_in.at[source],
            send_sem=sq_send.at[0],
            recv_sem=sq_recv.at[source],
            device_id={"mp": source},
            device_id_type=MESH,
        )

    def z_copy(s, c, way):
        part = pl.ds(c * rows, rows)
        dest, sems = (from_low, low_recv) if way > 0 else (from_high, high_recv)
        z = targets[s]
        return pltpu.make_async_remote_copy(
            src_ref=own.at[s, part],
            dst_ref=dest.at[z, part],
            send_sem=z_send.at[s, c],
            recv_sem=sems.at[z, c],
            device_id={"mp": (zm + way) * PAIRS + ym},
            device_id_type=MESH,
        )

    for s in range(lines):
        multiply(s, peer_out, s)
        if s == 0:
            pl.semaphore_wait(barrier, count - 1)
        for c in range(CHUNKS):
            y_copy(s, c).start()
        if s == 0:
            for d in range(1, count):
                sq_copy(d).start()
    for s in range(lines):
        multiply(lines + s, own, s)

    squares = squares_ref[...]
    for d in range(1, count):
        source = (me + d) % count
        sq_arrival(source).wait_recv()
        squares = squares + sq_in[source]
    inverse = 1.0 / jnp.sqrt(squares[0:1] / (count * gained_ref.shape[1]) + 1e-05)
    scaling = jnp.transpose(jnp.broadcast_to(inverse, (128, tokens)))

    for s in range(lines):
        z = targets[s]
        for c in range(CHUNKS):
            part = pl.ds(c * rows, rows)
            y_copy(s, c).wait_recv()
            total[...] = own[s, part, :].astype(jnp.float32) + peer_in[s, part, :].astype(
                jnp.float32
            )

            @pl.when(jnp.logical_and(z >= zm, zm > 0))
            def _():
                z_copy_in(z, c, from_low, low_recv, own, z_send, rows, zm - 1, ym).wait_recv()
                total[...] += from_low[z, part, :].astype(jnp.float32)

            @pl.when(jnp.logical_and(z <= zm, zm < lines - 1))
            def _():
                z_copy_in(z, c, from_high, high_recv, own, z_send, rows, zm + 1, ym).wait_recv()
                total[...] += from_high[z, part, :].astype(jnp.float32)

            if s < lines - 1:
                own[s, part, :] = total[...].astype(jnp.bfloat16)

                @pl.when(z > zm)
                def _():
                    z_copy(s, c, 1).start()

                @pl.when(z < zm)
                def _():
                    z_copy(s, c, -1).start()
            else:
                factor = scaling[c * rows : (c + 1) * rows]
                for k in range(width // 128):
                    cols = slice(k * 128, (k + 1) * 128)
                    out_ref[part, cols] = (total[:, cols] * factor).astype(jnp.bfloat16)

    for d in range(1, count):
        sq_copy(d).wait_send()
    for s in range(lines):
        z = targets[s]
        for c in range(CHUNKS):
            y_copy(s, c).wait_send()
            if s < lines - 1:

                @pl.when(z > zm)
                def _():
                    z_copy(s, c, 1).wait_send()

                @pl.when(z < zm)
                def _():
                    z_copy(s, c, -1).wait_send()


def z_copy_in(z, c, dest, sems, own, z_send, rows, near, ym):
    part = pl.ds(c * rows, rows)
    return pltpu.make_async_remote_copy(
        src_ref=own.at[0, part],
        dst_ref=dest.at[z, part],
        send_sem=z_send.at[0, c],
        recv_sem=sems.at[z, c],
        device_id={"mp": near * PAIRS + ym},
        device_id_type=MESH,
    )


def project(gained, squares, weight):
    tokens, depth = gained.shape
    count = lax.axis_size("mp")
    lines = count // PAIRS
    width = weight.shape[1] // count
    dma = pltpu.SemaphoreType.DMA
    block = lambda n: pltpu.VMEM((n, tokens, width), jnp.bfloat16)
    return pl.pallas_call(
        project_kernel,
        out_shape=jax.ShapeDtypeStruct((tokens, width), jnp.bfloat16),
        in_specs=[
            pl.BlockSpec(memory_space=pltpu.VMEM),
            pl.BlockSpec(memory_space=pltpu.VMEM),
            pl.BlockSpec(memory_space=pl.ANY),
        ],
        out_specs=pl.BlockSpec(memory_space=pltpu.VMEM),
        scratch_shapes=[
            pltpu.VMEM((2 * lines, depth, width), jnp.bfloat16),
            block(lines),
            block(lines),
            block(lines),
            block(lines),
            block(lines),
            pltpu.VMEM((tokens // CHUNKS, width), jnp.float32),
            pltpu.VMEM((count, 8, tokens), jnp.float32),
            dma((2 * lines,)),
            dma((lines, CHUNKS)),
            dma((lines, CHUNKS)),
            dma((lines, CHUNKS)),
            dma((lines, CHUNKS)),
            dma((lines, CHUNKS)),
            dma((count,)),
            dma((count,)),
        ],
        compiler_params=pltpu.CompilerParams(
            collective_id=0, has_side_effects=True, vmem_limit_bytes=56 << 20
        ),
        cost_estimate=pl.CostEstimate(
            flops=2 * tokens * depth * width * count,
            bytes_accessed=2 * depth * width * count,
            transcendentals=0,
        ),
        name="project",
    )(gained, squares, weight)


def solution(mesh):
    placed = (
        P("seq", "mp"),
        P("seq", "mp"),
        P("seq", None),
        P("seq", None),
        P("seq", "mp"),
        P("seq", "mp"),
        P("mp"),
        P("mp"),
        P("mp", None),
    )
    return jax.shard_map(
        on_device, mesh=mesh, in_specs=placed, out_specs=P("seq", "mp"), check_vma=False
    )
```

```python
import jax
import jax.numpy as jnp
from jax import lax
from jax.experimental import pallas as pl
from jax.experimental.pallas import tpu as pltpu
from jax.sharding import PartitionSpec as P

BLOCK = 256
PAIRS = 2
CHUNKS = 4
RELAY_CHUNKS = 2
LANES = 128
MESH = pl.DeviceIdType.MESH
EXACT = lax.Precision.HIGHEST


def step_target(step, zm, lines):
    up = zm // (lines // 2)
    near = zm * (1 - up) + (lines - 1 - zm) * up
    if step == lines - 1:
        return zm
    turned = (step + near) // (lines - 1)
    seen = (lines - 1 - step) * (1 - turned) + (step - (lines - 1 - near)) * turned
    return seen * (1 - up) + (lines - 1 - seen) * up


def layer_kernel(
    signal_ref,
    gate_ref,
    keys_ref,
    query_ref,
    decay_ref,
    step_ref,
    skip_ref,
    gain_ref,
    weight_ref,
    out_ref,
    gained_ref,
    squares_ref,
    inner,
    local,
    spread,
    relay_out,
    relay_in,
    square_sum,
    wbuf,
    peer_out,
    peer_in,
    own,
    from_low,
    from_high,
    total,
    sq_in,
    w_sem,
    y_send,
    y_recv,
    z_send,
    low_recv,
    high_recv,
    sq_send,
    sq_recv,
    relay_send,
    relay_recv,
):
    me = lax.axis_index("mp")
    lines = own.shape[0]
    count = lines * PAIRS
    zm = me // PAIRS
    ym = me % PAIRS
    tokens = gained_ref.shape[0]
    width = out_ref.shape[1]
    rows = tokens // CHUNKS
    tile = min(256, width)

    barrier = pltpu.get_barrier_semaphore()
    for d in range(1, count):
        pl.semaphore_signal(
            barrier, inc=1, device_id={"mp": (me + d) % count}, device_id_type=MESH
        )

    seq = lax.axis_index("seq")
    seq_count = lax.axis_size("seq")
    for d in (1, seq_count - 1):
        pl.semaphore_signal(
            barrier, inc=1, device_id={"seq": (seq + d) % seq_count}, device_id_type=MESH
        )

    targets = [step_target(s, zm, lines) for s in range(lines)]
    columns = [z * PAIRS + 1 - ym for z in targets] + [z * PAIRS + ym for z in targets]

    def w_copy(t):
        cols = pl.ds(pl.multiple_of(columns[t] * width, width), width)
        return pltpu.make_async_copy(weight_ref.at[:, cols], wbuf.at[t], w_sem.at[t])

    for t in range(2 * lines):
        w_copy(t).start()

    heads = decay_ref.shape[0]
    width_in = signal_ref.shape[1]
    head_width = width_in // heads
    state_width = keys_ref.shape[1]
    blocks = tokens // BLOCK
    half = BLOCK // 2
    row_ids = lax.broadcasted_iota(jnp.int32, (BLOCK, BLOCK), 0)
    col_ids = lax.broadcasted_iota(jnp.int32, (BLOCK, BLOCK), 1)
    upper = jnp.where(row_ids <= col_ids, 1.0, 0.0).astype(jnp.float32)
    barred = jnp.where(row_ids >= col_ids, 0.0, -1e30).astype(jnp.float32)
    low_lane = lax.broadcasted_iota(jnp.int32, (half, LANES), 1) < head_width
    slot_ids = lax.broadcasted_iota(jnp.int32, (LANES, width_in), 0)
    head_ids = lax.broadcasted_iota(jnp.int32, (LANES, width_in), 1) // head_width
    pick_feed = jnp.where(slot_ids == head_ids + heads, 1.0, 0.0).astype(jnp.float32)
    pick_grow = jnp.where(slot_ids == head_ids + 2 * heads, 1.0, 0.0).astype(jnp.float32)

    cum_rows, cum_cols = [], []
    for b in range(blocks):
        span = slice(b * BLOCK, (b + 1) * BLOCK)
        cum_t = jnp.dot(
            decay_ref[:, span], upper, precision=EXACT, preferred_element_type=jnp.float32
        )
        feed_t = step_ref[:, span] * jnp.exp(cum_t[:, BLOCK - 1 : BLOCK] - cum_t)
        filler = jnp.zeros((LANES - 3 * heads, BLOCK), jnp.float32)
        cols = jnp.transpose(jnp.concatenate([cum_t, feed_t, jnp.exp(cum_t), filler], axis=0))
        cum_rows.append(cum_t)
        cum_cols.append(cols)
        feed = jnp.dot(cols, pick_feed, precision=EXACT, preferred_element_type=jnp.float32)
        spread[span, :] = jnp.dot(
            cols, pick_grow, precision=EXACT, preferred_element_type=jnp.float32
        )
        feed_rows = (signal_ref[span, :].astype(jnp.float32) * feed).astype(jnp.bfloat16)
        keys_t = jnp.transpose(keys_ref[span, :].astype(jnp.float32)).astype(jnp.bfloat16)
        local[b] = jnp.dot(keys_t, feed_rows, preferred_element_type=jnp.float32)

    def block_decay(b):
        last = (b + 1) * BLOCK - 1
        return spread[last : last + 1, :]

    def relay_copy(c):
        part = pl.ds(c * (state_width // RELAY_CHUNKS), state_width // RELAY_CHUNKS)
        return pltpu.make_async_remote_copy(
            src_ref=relay_out.at[part],
            dst_ref=relay_in.at[part],
            send_sem=relay_send.at[c],
            recv_sem=relay_recv.at[c],
            device_id={"seq": (seq + 1) % seq_count},
            device_id_type=MESH,
        )

    pl.semaphore_wait(barrier, count + 1)

    @pl.when(seq == 0)
    def _():
        relay_in[...] = jnp.zeros_like(relay_in)

    def relay():
        for c in range(RELAY_CHUNKS):
            n = state_width // RELAY_CHUNKS
            part = slice(c * n, (c + 1) * n)

            @pl.when(seq > 0)
            def _():
                relay_copy(c).wait_recv()

            @pl.when(seq < seq_count - 1)
            def _():
                state = relay_in[part, :].astype(jnp.float32)
                for b in range(blocks):
                    state = block_decay(b) * state + local[b, part, :]
                relay_out[part, :] = state.astype(jnp.bfloat16)
                relay_copy(c).start()

    def inner_pair(b, p, scores):
        cols = slice(p * LANES, (p + 1) * LANES)
        base = b * BLOCK
        signal_pair = signal_ref[base : base + BLOCK, cols]
        parts = []
        for top, wide in ((0, half), (half, BLOCK)):
            outs = []
            for h in (2 * p, 2 * p + 1):
                gaps = (
                    cum_cols[b][top : top + half, h : h + 1]
                    - cum_rows[b][h : h + 1, :wide]
                    + barred[top : top + half, :wide]
                )
                scaled = scores[top : top + half, :wide] * jnp.exp(gaps)
                scaled = scaled * step_ref[h : h + 1, base : base + wide]
                outs.append(
                    jnp.dot(
                        scaled.astype(jnp.bfloat16),
                        signal_pair[:wide],
                        preferred_element_type=jnp.float32,
                    )
                )
            parts.append(jnp.where(low_lane, outs[0], outs[1]))
        for number, value in enumerate(parts):
            at = slice(base + number * half, base + (number + 1) * half)
            inner[at, cols] = value + skip_ref[:, cols] * signal_ref[at, cols].astype(jnp.float32)

    turn = 0
    pair_count = width_in // LANES
    every = max(1, blocks * pair_count // 3)
    done = 0
    for b in range(blocks):
        span = slice(b * BLOCK, (b + 1) * BLOCK)
        scores = lax.dot_general(
            query_ref[span, :],
            keys_ref[span, :],
            (((1,), (1,)), ((), ())),
            preferred_element_type=jnp.float32,
        )
        for p in range(pair_count):
            if done % every == 0 and turn < 3:
                pl.when(seq == turn)(relay)
                turn += 1
            inner_pair(b, p, scores)
            done += 1
    pl.when(seq >= turn)(relay)

    state = relay_in[...].astype(jnp.float32)
    for b in range(blocks):
        span = slice(b * BLOCK, (b + 1) * BLOCK)
        carried = state.astype(jnp.bfloat16)
        squared = jnp.zeros((BLOCK, LANES), jnp.float32)
        for p in range(pair_count):
            cols = slice(p * LANES, (p + 1) * LANES)
            read = jnp.dot(query_ref[span, :], carried[:, cols], preferred_element_type=jnp.float32)
            gate = gate_ref[span, cols].astype(jnp.float32)
            gated = (inner[span, cols] + spread[span, cols] * read) * (gate / (1.0 + jnp.exp(-gate)))
            squared = squared + gated * gated
            gained_ref[span, cols] = (gated * gain_ref[:, cols]).astype(jnp.bfloat16)
        square_sum[span, :] = squared
        if b < blocks - 1:
            state = block_decay(b) * state + local[b]
    total_row = jnp.sum(jnp.transpose(square_sum[...]), axis=0, keepdims=True)
    squares_ref[...] = jnp.broadcast_to(total_row, (8, tokens))

    def multiply(t, dest, slot):
        w_copy(t).wait()

        @pl.loop(0, width // tile)
        def _(i):
            cols = pl.ds(pl.multiple_of(i * tile, tile), tile)
            dest[slot, :, cols] = jnp.dot(
                gained_ref[...], wbuf[t, :, cols], preferred_element_type=jnp.float32
            ).astype(jnp.bfloat16)

    def y_copy(s, c):
        part = pl.ds(c * rows, rows)
        return pltpu.make_async_remote_copy(
            src_ref=peer_out.at[s, part],
            dst_ref=peer_in.at[s, part],
            send_sem=y_send.at[s, c],
            recv_sem=y_recv.at[s, c],
            device_id={"mp": zm * PAIRS + 1 - ym},
            device_id_type=MESH,
        )

    def sq_copy(d):
        return pltpu.make_async_remote_copy(
            src_ref=squares_ref,
            dst_ref=sq_in.at[me],
            send_sem=sq_send.at[d],
            recv_sem=sq_recv.at[me],
            device_id={"mp": (me + d) % count},
            device_id_type=MESH,
        )

    def sq_arrival(source):
        return pltpu.make_async_remote_copy(
            src_ref=squares_ref,
            dst_ref=sq_in.at[source],
            send_sem=sq_send.at[0],
            recv_sem=sq_recv.at[source],
            device_id={"mp": source},
            device_id_type=MESH,
        )

    def z_copy(s, c, way):
        part = pl.ds(c * rows, rows)
        dest, sems = (from_low, low_recv) if way > 0 else (from_high, high_recv)
        z = targets[s]
        return pltpu.make_async_remote_copy(
            src_ref=own.at[s, part],
            dst_ref=dest.at[z, part],
            send_sem=z_send.at[s, c],
            recv_sem=sems.at[z, c],
            device_id={"mp": (zm + way) * PAIRS + ym},
            device_id_type=MESH,
        )

    for s in range(lines):
        multiply(s, peer_out, s)
        for c in range(CHUNKS):
            y_copy(s, c).start()
        if s == 0:
            for d in range(1, count):
                sq_copy(d).start()
    for s in range(lines):
        multiply(lines + s, own, s)

    squares = squares_ref[...]
    for d in range(1, count):
        source = (me + d) % count
        sq_arrival(source).wait_recv()
        squares = squares + sq_in[source]
    inverse = 1.0 / jnp.sqrt(squares[0:1] / (count * gained_ref.shape[1]) + 1e-05)
    scaling = jnp.transpose(jnp.broadcast_to(inverse, (128, tokens)))

    for s in range(lines):
        z = targets[s]
        for c in range(CHUNKS):
            part = pl.ds(c * rows, rows)
            y_copy(s, c).wait_recv()
            total[...] = own[s, part, :].astype(jnp.float32) + peer_in[s, part, :].astype(
                jnp.float32
            )

            @pl.when(jnp.logical_and(z >= zm, zm > 0))
            def _():
                z_copy_in(z, c, from_low, low_recv, own, z_send, rows, zm - 1, ym).wait_recv()
                total[...] += from_low[z, part, :].astype(jnp.float32)

            @pl.when(jnp.logical_and(z <= zm, zm < lines - 1))
            def _():
                z_copy_in(z, c, from_high, high_recv, own, z_send, rows, zm + 1, ym).wait_recv()
                total[...] += from_high[z, part, :].astype(jnp.float32)

            if s < lines - 1:
                own[s, part, :] = total[...].astype(jnp.bfloat16)

                @pl.when(z > zm)
                def _():
                    z_copy(s, c, 1).start()

                @pl.when(z < zm)
                def _():
                    z_copy(s, c, -1).start()
            else:
                factor = scaling[c * rows : (c + 1) * rows]
                for k in range(width // 128):
                    cols = slice(k * 128, (k + 1) * 128)
                    out_ref[part, cols] = (total[:, cols] * factor).astype(jnp.bfloat16)

    @pl.when(seq < seq_count - 1)
    def _():
        for c in range(RELAY_CHUNKS):
            relay_copy(c).wait_send()

    for d in range(1, count):
        sq_copy(d).wait_send()
    for s in range(lines):
        z = targets[s]
        for c in range(CHUNKS):
            y_copy(s, c).wait_send()
            if s < lines - 1:

                @pl.when(z > zm)
                def _():
                    z_copy(s, c, 1).wait_send()

                @pl.when(z < zm)
                def _():
                    z_copy(s, c, -1).wait_send()


def z_copy_in(z, c, dest, sems, own, z_send, rows, near, ym):
    part = pl.ds(c * rows, rows)
    return pltpu.make_async_remote_copy(
        src_ref=own.at[0, part],
        dst_ref=dest.at[z, part],
        send_sem=z_send.at[0, c],
        recv_sem=sems.at[z, c],
        device_id={"mp": near * PAIRS + ym},
        device_id_type=MESH,
    )


def on_device(
    signal,
    gate_input,
    input_map,
    output_map,
    log_decay,
    step_size,
    skip_gain,
    norm_gain,
    out_weight,
):
    tokens, depth = signal.shape
    heads = log_decay.shape[1]
    state_width = input_map.shape[1]
    count = lax.axis_size("mp")
    lines = count // PAIRS
    width = out_weight.shape[1] // count
    skip_lanes = jnp.repeat(skip_gain, depth // heads)[None]
    dma = pltpu.SemaphoreType.DMA
    held = lambda n: pltpu.VMEM((n, tokens, width), jnp.bfloat16)
    whole = pl.BlockSpec(memory_space=pltpu.VMEM)
    return pl.pallas_call(
        layer_kernel,
        out_shape=jax.ShapeDtypeStruct((tokens, width), jnp.bfloat16),
        in_specs=[whole] * 8 + [pl.BlockSpec(memory_space=pl.ANY)],
        out_specs=whole,
        scratch_shapes=[
            pltpu.VMEM((tokens, depth), jnp.bfloat16),
            pltpu.VMEM((8, tokens), jnp.float32),
            pltpu.VMEM((tokens, depth), jnp.float32),
            pltpu.VMEM((tokens // BLOCK, state_width, depth), jnp.float32),
            pltpu.VMEM((tokens, depth), jnp.float32),
            pltpu.VMEM((state_width, depth), jnp.bfloat16),
            pltpu.VMEM((state_width, depth), jnp.bfloat16),
            pltpu.VMEM((tokens, LANES), jnp.float32),
            pltpu.VMEM((2 * lines, depth, width), jnp.bfloat16),
            held(lines),
            held(lines),
            held(lines),
            held(lines),
            held(lines),
            pltpu.VMEM((tokens // CHUNKS, width), jnp.float32),
            pltpu.VMEM((count, 8, tokens), jnp.float32),
            dma((2 * lines,)),
            dma((lines, CHUNKS)),
            dma((lines, CHUNKS)),
            dma((lines, CHUNKS)),
            dma((lines, CHUNKS)),
            dma((lines, CHUNKS)),
            dma((count,)),
            dma((count,)),
            dma((RELAY_CHUNKS,)),
            dma((RELAY_CHUNKS,)),
        ],
        compiler_params=pltpu.CompilerParams(
            collective_id=0, has_side_effects=True, vmem_limit_bytes=58 << 20
        ),
        name="layer",
    )(
        signal,
        gate_input,
        input_map,
        output_map,
        jnp.transpose(log_decay),
        jnp.transpose(step_size),
        skip_lanes,
        norm_gain[None],
        out_weight,
    )


def solution(mesh):
    placed = (
        P("seq", "mp"),
        P("seq", "mp"),
        P("seq", None),
        P("seq", None),
        P("seq", "mp"),
        P("seq", "mp"),
        P("mp"),
        P("mp"),
        P("mp", None),
    )
    return jax.shard_map(
        on_device, mesh=mesh, in_specs=placed, out_specs=P("seq", "mp"), check_vma=False
    )
```

```python
import jax
import jax.numpy as jnp
from jax import lax
from jax.experimental import pallas as pl
from jax.experimental.pallas import tpu as pltpu
from jax.sharding import PartitionSpec as P

BLOCK = 256
PAIRS = 2
CHUNKS = 4
RELAY_CHUNKS = 2
LINE_SHARE = 8
LANES = 128
MESH = pl.DeviceIdType.MESH
EXACT = lax.Precision.HIGHEST


def step_target(step, zm, lines):
    up = zm // (lines // 2)
    near = zm * (1 - up) + (lines - 1 - zm) * up
    if step == lines - 1:
        return zm
    turned = (step + near) // (lines - 1)
    seen = (lines - 1 - step) * (1 - turned) + (step - (lines - 1 - near)) * turned
    return seen * (1 - up) + (lines - 1 - seen) * up


def layer_kernel(
    signal_ref,
    gate_ref,
    keys_ref,
    query_ref,
    decay_ref,
    step_ref,
    skip_ref,
    gain_ref,
    weight_ref,
    out_ref,
    gained_ref,
    squares_ref,
    inner,
    local,
    spread,
    relay_out,
    relay_in,
    square_sum,
    line_total,
    line_low,
    line_high,
    wbuf,
    peer_out,
    peer_in,
    own,
    from_low,
    from_high,
    total,
    sq_in,
    w_sem,
    y_send,
    y_recv,
    z_send,
    low_recv,
    high_recv,
    sq_send,
    sq_recv,
    relay_send,
    relay_recv,
    line_send,
    line_low_recv,
    line_high_recv,
    cross_send,
    cross_recv,
):
    me = lax.axis_index("mp")
    lines = own.shape[0]
    count = lines * PAIRS
    zm = me // PAIRS
    ym = me % PAIRS
    tokens = gained_ref.shape[0]
    width = out_ref.shape[1]
    line_rows = tokens // LINE_SHARE
    rows = (tokens - line_rows) // CHUNKS
    line_part = pl.ds(tokens - line_rows, line_rows)
    tile = min(256, width)

    barrier = pltpu.get_barrier_semaphore()
    for d in range(1, count):
        pl.semaphore_signal(
            barrier, inc=1, device_id={"mp": (me + d) % count}, device_id_type=MESH
        )

    seq = lax.axis_index("seq")
    seq_count = lax.axis_size("seq")
    for d in (1, seq_count - 1):
        pl.semaphore_signal(
            barrier, inc=1, device_id={"seq": (seq + d) % seq_count}, device_id_type=MESH
        )

    targets = [step_target(s, zm, lines) for s in range(lines)]
    columns = [z * PAIRS + 1 - ym for z in targets] + [z * PAIRS + ym for z in targets]

    def w_copy(t):
        cols = pl.ds(pl.multiple_of(columns[t] * width, width), width)
        return pltpu.make_async_copy(weight_ref.at[:, cols], wbuf.at[t], w_sem.at[t])

    for t in range(2 * lines):
        w_copy(t).start()

    heads = decay_ref.shape[0]
    width_in = signal_ref.shape[1]
    head_width = width_in // heads
    state_width = keys_ref.shape[1]
    blocks = tokens // BLOCK
    half = BLOCK // 2
    row_ids = lax.broadcasted_iota(jnp.int32, (BLOCK, BLOCK), 0)
    col_ids = lax.broadcasted_iota(jnp.int32, (BLOCK, BLOCK), 1)
    upper = jnp.where(row_ids <= col_ids, 1.0, 0.0).astype(jnp.float32)
    barred = jnp.where(row_ids >= col_ids, 0.0, -1e30).astype(jnp.float32)
    low_lane = lax.broadcasted_iota(jnp.int32, (half, LANES), 1) < head_width
    slot_ids = lax.broadcasted_iota(jnp.int32, (LANES, width_in), 0)
    head_ids = lax.broadcasted_iota(jnp.int32, (LANES, width_in), 1) // head_width
    pick_feed = jnp.where(slot_ids == head_ids + heads, 1.0, 0.0).astype(jnp.float32)
    pick_grow = jnp.where(slot_ids == head_ids + 2 * heads, 1.0, 0.0).astype(jnp.float32)

    cum_rows, cum_cols = [], []
    for b in range(blocks):
        span = slice(b * BLOCK, (b + 1) * BLOCK)
        cum_t = jnp.dot(
            decay_ref[:, span], upper, precision=EXACT, preferred_element_type=jnp.float32
        )
        feed_t = step_ref[:, span] * jnp.exp(cum_t[:, BLOCK - 1 : BLOCK] - cum_t)
        filler = jnp.zeros((LANES - 3 * heads, BLOCK), jnp.float32)
        cols = jnp.transpose(jnp.concatenate([cum_t, feed_t, jnp.exp(cum_t), filler], axis=0))
        cum_rows.append(cum_t)
        cum_cols.append(cols)
        feed = jnp.dot(cols, pick_feed, precision=EXACT, preferred_element_type=jnp.float32)
        spread[span, :] = jnp.dot(
            cols, pick_grow, precision=EXACT, preferred_element_type=jnp.float32
        )
        feed_rows = (signal_ref[span, :].astype(jnp.float32) * feed).astype(jnp.bfloat16)
        keys_t = jnp.transpose(keys_ref[span, :].astype(jnp.float32)).astype(jnp.bfloat16)
        local[b] = jnp.dot(keys_t, feed_rows, preferred_element_type=jnp.float32)

    def block_decay(b):
        last = (b + 1) * BLOCK - 1
        return spread[last : last + 1, :]

    def relay_copy(c):
        part = pl.ds(c * (state_width // RELAY_CHUNKS), state_width // RELAY_CHUNKS)
        return pltpu.make_async_remote_copy(
            src_ref=relay_out.at[part],
            dst_ref=relay_in.at[part],
            send_sem=relay_send.at[c],
            recv_sem=relay_recv.at[c],
            device_id={"seq": (seq + 1) % seq_count},
            device_id_type=MESH,
        )

    pl.semaphore_wait(barrier, count + 1)

    @pl.when(seq == 0)
    def _():
        relay_in[...] = jnp.zeros_like(relay_in)

    def relay():
        for c in range(RELAY_CHUNKS):
            n = state_width // RELAY_CHUNKS
            part = slice(c * n, (c + 1) * n)

            @pl.when(seq > 0)
            def _():
                relay_copy(c).wait_recv()

            @pl.when(seq < seq_count - 1)
            def _():
                state = relay_in[part, :].astype(jnp.float32)
                for b in range(blocks):
                    state = block_decay(b) * state + local[b, part, :]
                relay_out[part, :] = state.astype(jnp.bfloat16)
                relay_copy(c).start()

    def inner_pair(b, p, scores):
        cols = slice(p * LANES, (p + 1) * LANES)
        base = b * BLOCK
        signal_pair = signal_ref[base : base + BLOCK, cols]
        parts = []
        for top, wide in ((0, half), (half, BLOCK)):
            outs = []
            for h in (2 * p, 2 * p + 1):
                gaps = (
                    cum_cols[b][top : top + half, h : h + 1]
                    - cum_rows[b][h : h + 1, :wide]
                    + barred[top : top + half, :wide]
                )
                scaled = scores[top : top + half, :wide] * jnp.exp(gaps)
                scaled = scaled * step_ref[h : h + 1, base : base + wide]
                outs.append(
                    jnp.dot(
                        scaled.astype(jnp.bfloat16),
                        signal_pair[:wide],
                        preferred_element_type=jnp.float32,
                    )
                )
            parts.append(jnp.where(low_lane, outs[0], outs[1]))
        for number, value in enumerate(parts):
            at = slice(base + number * half, base + (number + 1) * half)
            inner[at, cols] = value + jnp.where(
                low_lane, skip_ref[2 * p], skip_ref[2 * p + 1]
            ) * signal_ref[at, cols].astype(jnp.float32)

    turn = 0
    pair_count = width_in // LANES
    every = max(1, blocks * pair_count // 3)
    done = 0
    for b in range(blocks):
        span = slice(b * BLOCK, (b + 1) * BLOCK)
        scores = lax.dot_general(
            query_ref[span, :],
            keys_ref[span, :],
            (((1,), (1,)), ((), ())),
            preferred_element_type=jnp.float32,
        )
        for p in range(pair_count):
            if done % every == 0 and turn < 3:
                pl.when(seq == turn)(relay)
                turn += 1
            inner_pair(b, p, scores)
            done += 1
    pl.when(seq >= turn)(relay)

    def multiply(t, dest, slot, part):
        @pl.loop(0, width // tile)
        def _(i):
            cols = pl.ds(pl.multiple_of(i * tile, tile), tile)
            dest[slot, part, cols] = jnp.dot(
                gained_ref[part, :], wbuf[t, :, cols], preferred_element_type=jnp.float32
            ).astype(jnp.bfloat16)

    def y_copy(s, c):
        part = pl.ds(c * rows, rows)
        return pltpu.make_async_remote_copy(
            src_ref=peer_out.at[s, part],
            dst_ref=peer_in.at[s, part],
            send_sem=y_send.at[s, c],
            recv_sem=y_recv.at[s, c],
            device_id={"mp": zm * PAIRS + 1 - ym},
            device_id_type=MESH,
        )

    sent = 0
    state = relay_in[...].astype(jnp.float32)
    for b in range(blocks):
        span = slice(b * BLOCK, (b + 1) * BLOCK)
        carried = state.astype(jnp.bfloat16)
        squared = jnp.zeros((BLOCK, LANES), jnp.float32)
        for p in range(pair_count):
            cols = slice(p * LANES, (p + 1) * LANES)
            read = jnp.dot(query_ref[span, :], carried[:, cols], preferred_element_type=jnp.float32)
            gate = gate_ref[span, cols].astype(jnp.float32)
            gated = (inner[span, cols] + spread[span, cols] * read) * (gate / (1.0 + jnp.exp(-gate)))
            squared = squared + gated * gated
            gained_ref[span, cols] = (gated * gain_ref[:, cols]).astype(jnp.bfloat16)
        square_sum[span, :] = squared
        if b == 0:
            w_copy(0).wait()
        multiply(0, peer_out, 0, span)
        while sent < CHUNKS and (sent + 1) * rows <= (b + 1) * BLOCK:
            y_copy(0, sent).start()
            sent += 1
        if b < blocks - 1:
            state = block_decay(b) * state + local[b]
    total_row = jnp.sum(jnp.transpose(square_sum[...]), axis=0, keepdims=True)
    squares_ref[...] = jnp.broadcast_to(total_row, (8, tokens))

    def sq_copy(d):
        return pltpu.make_async_remote_copy(
            src_ref=squares_ref,
            dst_ref=sq_in.at[me],
            send_sem=sq_send.at[d],
            recv_sem=sq_recv.at[me],
            device_id={"mp": (me + d) % count},
            device_id_type=MESH,
        )

    def sq_arrival(source):
        return pltpu.make_async_remote_copy(
            src_ref=squares_ref,
            dst_ref=sq_in.at[source],
            send_sem=sq_send.at[0],
            recv_sem=sq_recv.at[source],
            device_id={"mp": source},
            device_id_type=MESH,
        )

    def z_copy(s, c, way):
        part = pl.ds(c * rows, rows)
        dest, sems = (from_low, low_recv) if way > 0 else (from_high, high_recv)
        z = targets[s]
        return pltpu.make_async_remote_copy(
            src_ref=own.at[s, part],
            dst_ref=dest.at[z, part],
            send_sem=z_send.at[s, c],
            recv_sem=sems.at[z, c],
            device_id={"mp": (zm + way) * PAIRS + ym},
            device_id_type=MESH,
        )

    for d in range(1, count):
        sq_copy(d).start()

    def line_copy(s, e, way):
        dest = ((from_low, line_low), (from_high, line_high))[way < 0][e]
        sems = line_low_recv if way > 0 else line_high_recv
        z = targets[s]
        return pltpu.make_async_remote_copy(
            src_ref=(own, peer_out)[e].at[s, line_part],
            dst_ref=dest.at[z, line_part] if e == 0 else dest.at[z],
            send_sem=line_send.at[s, e],
            recv_sem=sems.at[z, e],
            device_id={"mp": (zm + way) * PAIRS + ym},
            device_id_type=MESH,
        )

    def line_arrival(s, e, way):
        dest = ((from_low, line_low), (from_high, line_high))[way < 0][e]
        sems = line_low_recv if way > 0 else line_high_recv
        z = targets[s]
        return pltpu.make_async_remote_copy(
            src_ref=(own, peer_out)[e].at[s, line_part],
            dst_ref=dest.at[z, line_part] if e == 0 else dest.at[z],
            send_sem=line_send.at[s, e],
            recv_sem=sems.at[z, e],
            device_id={"mp": (zm - way) * PAIRS + ym},
            device_id_type=MESH,
        )

    def cross_copy():
        return pltpu.make_async_remote_copy(
            src_ref=peer_out.at[lines - 1, line_part],
            dst_ref=peer_in.at[lines - 1, line_part],
            send_sem=cross_send.at[0],
            recv_sem=cross_recv.at[0],
            device_id={"mp": zm * PAIRS + 1 - ym},
            device_id_type=MESH,
        )

    def line_step(s):
        z = targets[s]
        for e in (1, 0):
            mine = (own, peer_out)[e]
            line_total[...] = mine[s, line_part, :].astype(jnp.float32)

            @pl.when(jnp.logical_and(z >= zm, zm > 0))
            def _():
                line_arrival(s, e, 1).wait_recv()
                came = from_low[z, line_part, :] if e == 0 else line_low[z]
                line_total[...] += came.astype(jnp.float32)

            @pl.when(jnp.logical_and(z <= zm, zm < lines - 1))
            def _():
                line_arrival(s, e, -1).wait_recv()
                came = from_high[z, line_part, :] if e == 0 else line_high[z]
                line_total[...] += came.astype(jnp.float32)

            if s < lines - 1:
                mine[s, line_part, :] = line_total[...].astype(jnp.bfloat16)

                @pl.when(z > zm)
                def _():
                    line_copy(s, e, 1).start()

                @pl.when(z < zm)
                def _():
                    line_copy(s, e, -1).start()
            elif e == 1:
                mine[s, line_part, :] = line_total[...].astype(jnp.bfloat16)
                cross_copy().start()

    everything = slice(0, tokens)
    for s in range(lines):
        if s > 0:
            w_copy(s).wait()
            multiply(s, peer_out, s, everything)
            for c in range(CHUNKS):
                y_copy(s, c).start()
        w_copy(lines + s).wait()
        multiply(lines + s, own, s, everything)

    squares = squares_ref[...]
    for d in range(1, count):
        source = (me + d) % count
        sq_arrival(source).wait_recv()
        squares = squares + sq_in[source]
    inverse = 1.0 / jnp.sqrt(squares[0:1] / (count * gained_ref.shape[1]) + 1e-05)
    scaling = jnp.transpose(jnp.broadcast_to(inverse, (128, tokens)))

    for s in range(lines):
        z = targets[s]
        for early in range(2 * s, min(2 * s + 2, lines)):
            line_step(early)
        for c in range(CHUNKS):
            part = pl.ds(c * rows, rows)
            y_copy(s, c).wait_recv()
            total[...] = own[s, part, :].astype(jnp.float32) + peer_in[s, part, :].astype(
                jnp.float32
            )

            @pl.when(jnp.logical_and(z >= zm, zm > 0))
            def _():
                z_copy_in(z, c, from_low, low_recv, own, z_send, rows, zm - 1, ym).wait_recv()
                total[...] += from_low[z, part, :].astype(jnp.float32)

            @pl.when(jnp.logical_and(z <= zm, zm < lines - 1))
            def _():
                z_copy_in(z, c, from_high, high_recv, own, z_send, rows, zm + 1, ym).wait_recv()
                total[...] += from_high[z, part, :].astype(jnp.float32)

            if s < lines - 1:
                own[s, part, :] = total[...].astype(jnp.bfloat16)

                @pl.when(z > zm)
                def _():
                    z_copy(s, c, 1).start()

                @pl.when(z < zm)
                def _():
                    z_copy(s, c, -1).start()
            else:
                factor = scaling[c * rows : (c + 1) * rows]
                for k in range(width // 128):
                    cols = slice(k * 128, (k + 1) * 128)
                    out_ref[part, cols] = (total[:, cols] * factor).astype(jnp.bfloat16)

    cross_copy().wait_recv()
    line_total[...] += peer_in[lines - 1, line_part, :].astype(jnp.float32)
    factor = scaling[tokens - line_rows :]
    for k in range(width // 128):
        cols = slice(k * 128, (k + 1) * 128)
        out_ref[line_part, cols] = (line_total[:, cols] * factor).astype(jnp.bfloat16)

    cross_copy().wait_send()
    for s in range(lines - 1):
        z = targets[s]
        for e in (0, 1):

            @pl.when(z > zm)
            def _():
                line_copy(s, e, 1).wait_send()

            @pl.when(z < zm)
            def _():
                line_copy(s, e, -1).wait_send()

    @pl.when(seq < seq_count - 1)
    def _():
        for c in range(RELAY_CHUNKS):
            relay_copy(c).wait_send()

    for d in range(1, count):
        sq_copy(d).wait_send()
    for s in range(lines):
        z = targets[s]
        for c in range(CHUNKS):
            y_copy(s, c).wait_send()
            if s < lines - 1:

                @pl.when(z > zm)
                def _():
                    z_copy(s, c, 1).wait_send()

                @pl.when(z < zm)
                def _():
                    z_copy(s, c, -1).wait_send()


def z_copy_in(z, c, dest, sems, own, z_send, rows, near, ym):
    part = pl.ds(c * rows, rows)
    return pltpu.make_async_remote_copy(
        src_ref=own.at[0, part],
        dst_ref=dest.at[z, part],
        send_sem=z_send.at[0, c],
        recv_sem=sems.at[z, c],
        device_id={"mp": near * PAIRS + ym},
        device_id_type=MESH,
    )


def on_device(
    signal,
    gate_input,
    input_map,
    output_map,
    log_decay,
    step_size,
    skip_gain,
    norm_gain,
    out_weight,
):
    tokens, depth = signal.shape
    state_width = input_map.shape[1]
    count = lax.axis_size("mp")
    lines = count // PAIRS
    line_rows = tokens // LINE_SHARE
    width = out_weight.shape[1] // count
    dma = pltpu.SemaphoreType.DMA
    held = lambda n: pltpu.VMEM((n, tokens, width), jnp.bfloat16)
    whole = pl.BlockSpec(memory_space=pltpu.VMEM)
    return pl.pallas_call(
        layer_kernel,
        out_shape=jax.ShapeDtypeStruct((tokens, width), jnp.bfloat16),
        in_specs=[whole] * 6
        + [pl.BlockSpec(memory_space=pltpu.SMEM), whole]
        + [pl.BlockSpec(memory_space=pl.ANY)],
        out_specs=whole,
        scratch_shapes=[
            pltpu.VMEM((tokens, depth), jnp.bfloat16),
            pltpu.VMEM((8, tokens), jnp.float32),
            pltpu.VMEM((tokens, depth), jnp.float32),
            pltpu.VMEM((tokens // BLOCK, state_width, depth), jnp.float32),
            pltpu.VMEM((tokens, depth), jnp.float32),
            pltpu.VMEM((state_width, depth), jnp.bfloat16),
            pltpu.VMEM((state_width, depth), jnp.bfloat16),
            pltpu.VMEM((tokens, LANES), jnp.float32),
            pltpu.VMEM((line_rows, width), jnp.float32),
            pltpu.VMEM((lines, line_rows, width), jnp.bfloat16),
            pltpu.VMEM((lines, line_rows, width), jnp.bfloat16),
            pltpu.VMEM((2 * lines, depth, width), jnp.bfloat16),
            held(lines),
            held(lines),
            held(lines),
            held(lines),
            held(lines),
            pltpu.VMEM(((tokens - line_rows) // CHUNKS, width), jnp.float32),
            pltpu.VMEM((count, 8, tokens), jnp.float32),
            dma((2 * lines,)),
            dma((lines, CHUNKS)),
            dma((lines, CHUNKS)),
            dma((lines, CHUNKS)),
            dma((lines, CHUNKS)),
            dma((lines, CHUNKS)),
            dma((count,)),
            dma((count,)),
            dma((RELAY_CHUNKS,)),
            dma((RELAY_CHUNKS,)),
            dma((lines, 2)),
            dma((lines, 2)),
            dma((lines, 2)),
            dma((1,)),
            dma((1,)),
        ],
        compiler_params=pltpu.CompilerParams(
            collective_id=0, has_side_effects=True, vmem_limit_bytes=58 << 20
        ),
        name="layer",
    )(
        signal,
        gate_input,
        input_map,
        output_map,
        jnp.transpose(log_decay),
        jnp.transpose(step_size),
        skip_gain,
        norm_gain[None],
        out_weight,
    )


def solution(mesh):
    placed = (
        P("seq", "mp"),
        P("seq", "mp"),
        P("seq", None),
        P("seq", None),
        P("seq", "mp"),
        P("seq", "mp"),
        P("mp"),
        P("mp"),
        P("mp", None),
    )
    return jax.shard_map(
        on_device, mesh=mesh, in_specs=placed, out_specs=P("seq", "mp"), check_vma=False
    )
```

```python
import jax
import jax.numpy as jnp
from jax import lax
from jax.experimental import pallas as pl
from jax.experimental.pallas import tpu as pltpu
from jax.sharding import PartitionSpec as P

BLOCK = 256
PAIRS = 2
CHUNKS = 4
RELAY_CHUNKS = 2
LINE_SHARE = 8
LANES = 128
MESH = pl.DeviceIdType.MESH
EXACT = lax.Precision.HIGHEST


def step_target(step, zm, lines):
    up = zm // (lines // 2)
    near = zm * (1 - up) + (lines - 1 - zm) * up
    if step == lines - 1:
        return zm
    turned = (step + near) // (lines - 1)
    seen = (lines - 1 - step) * (1 - turned) + (step - (lines - 1 - near)) * turned
    return seen * (1 - up) + (lines - 1 - seen) * up


def layer_kernel(
    signal_ref,
    gate_ref,
    keys_ref,
    query_ref,
    decay_ref,
    step_ref,
    skip_ref,
    gain_ref,
    weight_ref,
    out_ref,
    gained_ref,
    squares_ref,
    inner,
    local,
    spread,
    relay_out,
    relay_in,
    square_sum,
    line_total,
    line_low,
    line_high,
    wbuf,
    peer_out,
    peer_in,
    own,
    from_low,
    from_high,
    total,
    sq_in,
    w_sem,
    y_send,
    y_recv,
    z_send,
    low_recv,
    high_recv,
    sq_send,
    sq_recv,
    relay_send,
    relay_recv,
    line_send,
    line_low_recv,
    line_high_recv,
    cross_send,
    cross_recv,
):
    me = lax.axis_index("mp")
    lines = own.shape[0]
    count = lines * PAIRS
    zm = me // PAIRS
    ym = me % PAIRS
    tokens = gained_ref.shape[0]
    width = out_ref.shape[1]
    line_rows = tokens // LINE_SHARE
    rows = (tokens - line_rows) // CHUNKS
    line_part = pl.ds(tokens - line_rows, line_rows)
    tile = min(256, width)

    barrier = pltpu.get_barrier_semaphore()
    for d in range(1, count):
        pl.semaphore_signal(
            barrier, inc=1, device_id={"mp": (me + d) % count}, device_id_type=MESH
        )

    seq = lax.axis_index("seq")
    seq_count = lax.axis_size("seq")
    for d in (1, seq_count - 1):
        pl.semaphore_signal(
            barrier, inc=1, device_id={"seq": (seq + d) % seq_count}, device_id_type=MESH
        )

    targets = [step_target(s, zm, lines) for s in range(lines)]
    columns = [z * PAIRS + 1 - ym for z in targets] + [z * PAIRS + ym for z in targets]

    def w_copy(t):
        cols = pl.ds(pl.multiple_of(columns[t] * width, width), width)
        return pltpu.make_async_copy(weight_ref.at[:, cols], wbuf.at[t], w_sem.at[t])

    for t in range(lines):
        w_copy(t).start()
        w_copy(lines + t).start()

    heads = decay_ref.shape[0]
    width_in = signal_ref.shape[1]
    head_width = width_in // heads
    state_width = keys_ref.shape[1]
    blocks = tokens // BLOCK
    half = BLOCK // 2
    row_ids = lax.broadcasted_iota(jnp.int32, (BLOCK, BLOCK), 0)
    col_ids = lax.broadcasted_iota(jnp.int32, (BLOCK, BLOCK), 1)
    upper = jnp.where(row_ids <= col_ids, 1.0, 0.0).astype(jnp.float32)
    barred = jnp.where(row_ids >= col_ids, 0.0, -1e30).astype(jnp.float32)
    low_lane = lax.broadcasted_iota(jnp.int32, (half, LANES), 1) < head_width
    slot_ids = lax.broadcasted_iota(jnp.int32, (LANES, width_in), 0)
    head_ids = lax.broadcasted_iota(jnp.int32, (LANES, width_in), 1) // head_width
    pick_feed = jnp.where(slot_ids == head_ids + heads, 1.0, 0.0).astype(jnp.float32)
    pick_grow = jnp.where(slot_ids == head_ids + 2 * heads, 1.0, 0.0).astype(jnp.float32)

    cum_rows, cum_cols = [], []
    for b in range(blocks):
        span = slice(b * BLOCK, (b + 1) * BLOCK)
        cum_t = jnp.dot(
            decay_ref[:, span], upper, precision=EXACT, preferred_element_type=jnp.float32
        )
        feed_t = step_ref[:, span] * jnp.exp(cum_t[:, BLOCK - 1 : BLOCK] - cum_t)
        filler = jnp.zeros((LANES - 3 * heads, BLOCK), jnp.float32)
        cols = jnp.transpose(jnp.concatenate([cum_t, feed_t, jnp.exp(cum_t), filler], axis=0))
        cum_rows.append(cum_t)
        cum_cols.append(cols)
        feed = jnp.dot(cols, pick_feed, precision=EXACT, preferred_element_type=jnp.float32)
        spread[span, :] = jnp.dot(
            cols, pick_grow, precision=EXACT, preferred_element_type=jnp.float32
        )
        feed_rows = (signal_ref[span, :].astype(jnp.float32) * feed).astype(jnp.bfloat16)
        keys_t = jnp.transpose(keys_ref[span, :].astype(jnp.float32)).astype(jnp.bfloat16)
        local[b] = jnp.dot(keys_t, feed_rows, preferred_element_type=jnp.float32)

    def block_decay(b):
        last = (b + 1) * BLOCK - 1
        return spread[last : last + 1, :]

    def relay_copy(c):
        part = pl.ds(c * (state_width // RELAY_CHUNKS), state_width // RELAY_CHUNKS)
        return pltpu.make_async_remote_copy(
            src_ref=relay_out.at[part],
            dst_ref=relay_in.at[part],
            send_sem=relay_send.at[c],
            recv_sem=relay_recv.at[c],
            device_id={"seq": (seq + 1) % seq_count},
            device_id_type=MESH,
        )

    pl.semaphore_wait(barrier, count + 1)

    @pl.when(seq == 0)
    def _():
        relay_in[...] = jnp.zeros_like(relay_in)

    def relay():
        for c in range(RELAY_CHUNKS):
            n = state_width // RELAY_CHUNKS
            part = slice(c * n, (c + 1) * n)

            @pl.when(seq > 0)
            def _():
                relay_copy(c).wait_recv()

            @pl.when(seq < seq_count - 1)
            def _():
                state = relay_in[part, :].astype(jnp.float32)
                for b in range(blocks):
                    state = block_decay(b) * state + local[b, part, :]
                relay_out[part, :] = state.astype(jnp.bfloat16)
                relay_copy(c).start()

    def inner_pair(b, p, scores):
        cols = slice(p * LANES, (p + 1) * LANES)
        base = b * BLOCK
        signal_pair = signal_ref[base : base + BLOCK, cols]
        parts = []
        for top, wide in ((0, half), (half, BLOCK)):
            outs = []
            for h in (2 * p, 2 * p + 1):
                gaps = (
                    cum_cols[b][top : top + half, h : h + 1]
                    - cum_rows[b][h : h + 1, :wide]
                    + barred[top : top + half, :wide]
                )
                scaled = scores[top : top + half, :wide] * jnp.exp(gaps)
                scaled = scaled * step_ref[h : h + 1, base : base + wide]
                outs.append(
                    jnp.dot(
                        scaled.astype(jnp.bfloat16),
                        signal_pair[:wide],
                        preferred_element_type=jnp.float32,
                    )
                )
            parts.append(jnp.where(low_lane, outs[0], outs[1]))
        for number, value in enumerate(parts):
            at = slice(base + number * half, base + (number + 1) * half)
            inner[at, cols] = value + jnp.where(
                low_lane, skip_ref[2 * p], skip_ref[2 * p + 1]
            ) * signal_ref[at, cols].astype(jnp.float32)

    turn = 0
    pair_count = width_in // LANES
    every = max(1, blocks * pair_count // 3)
    done = 0
    for b in range(blocks):
        span = slice(b * BLOCK, (b + 1) * BLOCK)
        scores = lax.dot_general(
            query_ref[span, :],
            keys_ref[span, :],
            (((1,), (1,)), ((), ())),
            preferred_element_type=jnp.float32,
        )
        for p in range(pair_count):
            if done % every == 0 and turn < 3:
                pl.when(seq == turn)(relay)
                turn += 1
            inner_pair(b, p, scores)
            done += 1
    pl.when(seq >= turn)(relay)

    def multiply(t, dest, slot, part):
        @pl.loop(0, width // tile)
        def _(i):
            cols = pl.ds(pl.multiple_of(i * tile, tile), tile)
            dest[slot, part, cols] = jnp.dot(
                gained_ref[part, :], wbuf[t, :, cols], preferred_element_type=jnp.float32
            ).astype(jnp.bfloat16)

    def y_copy(s, c):
        part = pl.ds(c * rows, rows)
        return pltpu.make_async_remote_copy(
            src_ref=peer_out.at[s, part],
            dst_ref=peer_in.at[s, part],
            send_sem=y_send.at[s, c],
            recv_sem=y_recv.at[s, c],
            device_id={"mp": zm * PAIRS + 1 - ym},
            device_id_type=MESH,
        )

    sent = 0
    state = relay_in[...].astype(jnp.float32)
    for b in range(blocks):
        span = slice(b * BLOCK, (b + 1) * BLOCK)
        carried = state.astype(jnp.bfloat16)
        squared = jnp.zeros((BLOCK, LANES), jnp.float32)
        for p in range(pair_count):
            cols = slice(p * LANES, (p + 1) * LANES)
            read = jnp.dot(query_ref[span, :], carried[:, cols], preferred_element_type=jnp.float32)
            gate = gate_ref[span, cols].astype(jnp.float32)
            gated = (inner[span, cols] + spread[span, cols] * read) * (gate / (1.0 + jnp.exp(-gate)))
            squared = squared + gated * gated
            gained_ref[span, cols] = (gated * gain_ref[:, cols]).astype(jnp.bfloat16)
        square_sum[span, :] = squared
        if b == 0:
            w_copy(0).wait()
        multiply(0, peer_out, 0, span)
        while sent < CHUNKS and (sent + 1) * rows <= (b + 1) * BLOCK:
            y_copy(0, sent).start()
            sent += 1
        if b < blocks - 1:
            state = block_decay(b) * state + local[b]
    total_row = jnp.sum(jnp.transpose(square_sum[...]), axis=0, keepdims=True)
    squares_ref[...] = jnp.broadcast_to(total_row, (8, tokens))

    def sq_copy(d):
        return pltpu.make_async_remote_copy(
            src_ref=squares_ref,
            dst_ref=sq_in.at[me],
            send_sem=sq_send.at[d],
            recv_sem=sq_recv.at[me],
            device_id={"mp": (me + d) % count},
            device_id_type=MESH,
        )

    def sq_arrival(source):
        return pltpu.make_async_remote_copy(
            src_ref=squares_ref,
            dst_ref=sq_in.at[source],
            send_sem=sq_send.at[0],
            recv_sem=sq_recv.at[source],
            device_id={"mp": source},
            device_id_type=MESH,
        )

    def z_copy(s, c, way):
        part = pl.ds(c * rows, rows)
        dest, sems = (from_low, low_recv) if way > 0 else (from_high, high_recv)
        z = targets[s]
        return pltpu.make_async_remote_copy(
            src_ref=own.at[s, part],
            dst_ref=dest.at[z, part],
            send_sem=z_send.at[s, c],
            recv_sem=sems.at[z, c],
            device_id={"mp": (zm + way) * PAIRS + ym},
            device_id_type=MESH,
        )

    for d in range(1, count):
        sq_copy(d).start()

    def line_copy(s, e, way):
        dest = ((from_low, line_low), (from_high, line_high))[way < 0][e]
        sems = line_low_recv if way > 0 else line_high_recv
        z = targets[s]
        return pltpu.make_async_remote_copy(
            src_ref=(own, peer_out)[e].at[s, line_part],
            dst_ref=dest.at[z, line_part] if e == 0 else dest.at[z],
            send_sem=line_send.at[s, e],
            recv_sem=sems.at[z, e],
            device_id={"mp": (zm + way) * PAIRS + ym},
            device_id_type=MESH,
        )

    def line_arrival(s, e, way):
        dest = ((from_low, line_low), (from_high, line_high))[way < 0][e]
        sems = line_low_recv if way > 0 else line_high_recv
        z = targets[s]
        return pltpu.make_async_remote_copy(
            src_ref=(own, peer_out)[e].at[s, line_part],
            dst_ref=dest.at[z, line_part] if e == 0 else dest.at[z],
            send_sem=line_send.at[s, e],
            recv_sem=sems.at[z, e],
            device_id={"mp": (zm - way) * PAIRS + ym},
            device_id_type=MESH,
        )

    def cross_copy():
        return pltpu.make_async_remote_copy(
            src_ref=peer_out.at[lines - 1, line_part],
            dst_ref=peer_in.at[lines - 1, line_part],
            send_sem=cross_send.at[0],
            recv_sem=cross_recv.at[0],
            device_id={"mp": zm * PAIRS + 1 - ym},
            device_id_type=MESH,
        )

    def line_step(s):
        z = targets[s]
        for e in (1, 0):
            mine = (own, peer_out)[e]
            line_total[...] = mine[s, line_part, :].astype(jnp.float32)

            @pl.when(jnp.logical_and(z >= zm, zm > 0))
            def _():
                line_arrival(s, e, 1).wait_recv()
                came = from_low[z, line_part, :] if e == 0 else line_low[z]
                line_total[...] += came.astype(jnp.float32)

            @pl.when(jnp.logical_and(z <= zm, zm < lines - 1))
            def _():
                line_arrival(s, e, -1).wait_recv()
                came = from_high[z, line_part, :] if e == 0 else line_high[z]
                line_total[...] += came.astype(jnp.float32)

            if s < lines - 1:
                mine[s, line_part, :] = line_total[...].astype(jnp.bfloat16)

                @pl.when(z > zm)
                def _():
                    line_copy(s, e, 1).start()

                @pl.when(z < zm)
                def _():
                    line_copy(s, e, -1).start()
            elif e == 1:
                mine[s, line_part, :] = line_total[...].astype(jnp.bfloat16)
                cross_copy().start()

    def feed_step(s):
        everything = slice(0, tokens)
        if s > 0:
            w_copy(s).wait()
            multiply(s, peer_out, s, everything)
            for c in range(CHUNKS):
                y_copy(s, c).start()
        w_copy(lines + s).wait()
        multiply(lines + s, own, s, everything)
        line_step(s)

    feed_step(0)
    feed_step(1)

    squares = squares_ref[...]
    for d in range(1, count):
        source = (me + d) % count
        sq_arrival(source).wait_recv()
        squares = squares + sq_in[source]
    inverse = 1.0 / jnp.sqrt(squares[0:1] / (count * gained_ref.shape[1]) + 1e-05)
    scaling = jnp.transpose(jnp.broadcast_to(inverse, (128, tokens)))

    for s in range(lines):
        z = targets[s]
        if 0 < s < lines - 1:
            feed_step(s + 1)
        for c in range(CHUNKS):
            part = pl.ds(c * rows, rows)
            y_copy(s, c).wait_recv()
            total[...] = own[s, part, :].astype(jnp.float32) + peer_in[s, part, :].astype(
                jnp.float32
            )

            @pl.when(jnp.logical_and(z >= zm, zm > 0))
            def _():
                z_copy_in(z, c, from_low, low_recv, own, z_send, rows, zm - 1, ym).wait_recv()
                total[...] += from_low[z, part, :].astype(jnp.float32)

            @pl.when(jnp.logical_and(z <= zm, zm < lines - 1))
            def _():
                z_copy_in(z, c, from_high, high_recv, own, z_send, rows, zm + 1, ym).wait_recv()
                total[...] += from_high[z, part, :].astype(jnp.float32)

            if s < lines - 1:
                own[s, part, :] = total[...].astype(jnp.bfloat16)

                @pl.when(z > zm)
                def _():
                    z_copy(s, c, 1).start()

                @pl.when(z < zm)
                def _():
                    z_copy(s, c, -1).start()
            else:
                factor = scaling[c * rows : (c + 1) * rows]
                for k in range(width // 128):
                    cols = slice(k * 128, (k + 1) * 128)
                    out_ref[part, cols] = (total[:, cols] * factor).astype(jnp.bfloat16)

    cross_copy().wait_recv()
    line_total[...] += peer_in[lines - 1, line_part, :].astype(jnp.float32)
    factor = scaling[tokens - line_rows :]
    for k in range(width // 128):
        cols = slice(k * 128, (k + 1) * 128)
        out_ref[line_part, cols] = (line_total[:, cols] * factor).astype(jnp.bfloat16)

    cross_copy().wait_send()
    for s in range(lines - 1):
        z = targets[s]
        for e in (0, 1):

            @pl.when(z > zm)
            def _():
                line_copy(s, e, 1).wait_send()

            @pl.when(z < zm)
            def _():
                line_copy(s, e, -1).wait_send()

    @pl.when(seq < seq_count - 1)
    def _():
        for c in range(RELAY_CHUNKS):
            relay_copy(c).wait_send()

    for d in range(1, count):
        sq_copy(d).wait_send()
    for s in range(lines):
        z = targets[s]
        for c in range(CHUNKS):
            y_copy(s, c).wait_send()
            if s < lines - 1:

                @pl.when(z > zm)
                def _():
                    z_copy(s, c, 1).wait_send()

                @pl.when(z < zm)
                def _():
                    z_copy(s, c, -1).wait_send()


def z_copy_in(z, c, dest, sems, own, z_send, rows, near, ym):
    part = pl.ds(c * rows, rows)
    return pltpu.make_async_remote_copy(
        src_ref=own.at[0, part],
        dst_ref=dest.at[z, part],
        send_sem=z_send.at[0, c],
        recv_sem=sems.at[z, c],
        device_id={"mp": near * PAIRS + ym},
        device_id_type=MESH,
    )


def on_device(
    signal,
    gate_input,
    input_map,
    output_map,
    log_decay,
    step_size,
    skip_gain,
    norm_gain,
    out_weight,
):
    tokens, depth = signal.shape
    state_width = input_map.shape[1]
    count = lax.axis_size("mp")
    lines = count // PAIRS
    line_rows = tokens // LINE_SHARE
    width = out_weight.shape[1] // count
    dma = pltpu.SemaphoreType.DMA
    held = lambda n: pltpu.VMEM((n, tokens, width), jnp.bfloat16)
    whole = pl.BlockSpec(memory_space=pltpu.VMEM)
    return pl.pallas_call(
        layer_kernel,
        out_shape=jax.ShapeDtypeStruct((tokens, width), jnp.bfloat16),
        in_specs=[whole] * 6
        + [pl.BlockSpec(memory_space=pltpu.SMEM), whole]
        + [pl.BlockSpec(memory_space=pl.ANY)],
        out_specs=whole,
        scratch_shapes=[
            pltpu.VMEM((tokens, depth), jnp.bfloat16),
            pltpu.VMEM((8, tokens), jnp.float32),
            pltpu.VMEM((tokens, depth), jnp.float32),
            pltpu.VMEM((tokens // BLOCK, state_width, depth), jnp.float32),
            pltpu.VMEM((tokens, depth), jnp.float32),
            pltpu.VMEM((state_width, depth), jnp.bfloat16),
            pltpu.VMEM((state_width, depth), jnp.bfloat16),
            pltpu.VMEM((tokens, LANES), jnp.float32),
            pltpu.VMEM((line_rows, width), jnp.float32),
            pltpu.VMEM((lines, line_rows, width), jnp.bfloat16),
            pltpu.VMEM((lines, line_rows, width), jnp.bfloat16),
            pltpu.VMEM((2 * lines, depth, width), jnp.bfloat16),
            held(lines),
            held(lines),
            held(lines),
            held(lines),
            held(lines),
            pltpu.VMEM(((tokens - line_rows) // CHUNKS, width), jnp.float32),
            pltpu.VMEM((count, 8, tokens), jnp.float32),
            dma((2 * lines,)),
            dma((lines, CHUNKS)),
            dma((lines, CHUNKS)),
            dma((lines, CHUNKS)),
            dma((lines, CHUNKS)),
            dma((lines, CHUNKS)),
            dma((count,)),
            dma((count,)),
            dma((RELAY_CHUNKS,)),
            dma((RELAY_CHUNKS,)),
            dma((lines, 2)),
            dma((lines, 2)),
            dma((lines, 2)),
            dma((1,)),
            dma((1,)),
        ],
        compiler_params=pltpu.CompilerParams(
            collective_id=0, has_side_effects=True, vmem_limit_bytes=58 << 20
        ),
        name="layer",
    )(
        signal,
        gate_input,
        input_map,
        output_map,
        jnp.transpose(log_decay),
        jnp.transpose(step_size),
        skip_gain,
        norm_gain[None],
        out_weight,
    )


def solution(mesh):
    placed = (
        P("seq", "mp"),
        P("seq", "mp"),
        P("seq", None),
        P("seq", None),
        P("seq", "mp"),
        P("seq", "mp"),
        P("mp"),
        P("mp"),
        P("mp", None),
    )
    return jax.shard_map(
        on_device, mesh=mesh, in_specs=placed, out_specs=P("seq", "mp"), check_vma=False
    )
```

```python
import jax
import jax.numpy as jnp
from jax import lax
from jax.experimental import pallas as pl
from jax.experimental.pallas import tpu as pltpu
from jax.sharding import PartitionSpec as P

BLOCK = 256
PAIRS = 2
CHUNKS = 7
RELAY_CHUNKS = 2
LINE_SHARE = 8
LANES = 128
MESH = pl.DeviceIdType.MESH
EXACT = lax.Precision.HIGHEST


def step_target(step, zm, lines):
    up = zm // (lines // 2)
    near = zm * (1 - up) + (lines - 1 - zm) * up
    if step == lines - 1:
        return zm
    turned = (step + near) // (lines - 1)
    seen = (lines - 1 - step) * (1 - turned) + (step - (lines - 1 - near)) * turned
    return seen * (1 - up) + (lines - 1 - seen) * up


def layer_kernel(
    signal_ref,
    gate_ref,
    keys_ref,
    query_ref,
    decay_ref,
    step_ref,
    skip_ref,
    gain_ref,
    weight_ref,
    out_ref,
    gained_ref,
    squares_ref,
    inner,
    local,
    spread,
    relay_out,
    relay_in,
    square_sum,
    line_total,
    line_low,
    line_high,
    wbuf,
    peer_out,
    peer_in,
    own,
    from_low,
    from_high,
    total,
    sq_in,
    w_sem,
    y_send,
    y_recv,
    z_send,
    low_recv,
    high_recv,
    sq_send,
    sq_recv,
    relay_send,
    relay_recv,
    line_send,
    line_low_recv,
    line_high_recv,
    cross_send,
    cross_recv,
):
    me = lax.axis_index("mp")
    lines = own.shape[0]
    count = lines * PAIRS
    zm = me // PAIRS
    ym = me % PAIRS
    tokens = gained_ref.shape[0]
    width = out_ref.shape[1]
    line_rows = tokens // LINE_SHARE
    rows = (tokens - line_rows) // CHUNKS
    line_part = pl.ds(tokens - line_rows, line_rows)
    tile = min(256, width)

    barrier = pltpu.get_barrier_semaphore()
    for d in range(1, count):
        pl.semaphore_signal(
            barrier, inc=1, device_id={"mp": (me + d) % count}, device_id_type=MESH
        )

    seq = lax.axis_index("seq")
    seq_count = lax.axis_size("seq")
    for d in (1, seq_count - 1):
        pl.semaphore_signal(
            barrier, inc=1, device_id={"seq": (seq + d) % seq_count}, device_id_type=MESH
        )

    targets = [step_target(s, zm, lines) for s in range(lines)]
    columns = [z * PAIRS + 1 - ym for z in targets] + [z * PAIRS + ym for z in targets]

    def w_copy(t):
        cols = pl.ds(pl.multiple_of(columns[t] * width, width), width)
        return pltpu.make_async_copy(weight_ref.at[:, cols], wbuf.at[t], w_sem.at[t])

    for t in range(lines):
        w_copy(t).start()
        w_copy(lines + t).start()

    heads = decay_ref.shape[0]
    width_in = signal_ref.shape[1]
    head_width = width_in // heads
    state_width = keys_ref.shape[1]
    blocks = tokens // BLOCK
    half = BLOCK // 2
    row_ids = lax.broadcasted_iota(jnp.int32, (BLOCK, BLOCK), 0)
    col_ids = lax.broadcasted_iota(jnp.int32, (BLOCK, BLOCK), 1)
    upper = jnp.where(row_ids <= col_ids, 1.0, 0.0).astype(jnp.float32)
    barred = jnp.where(row_ids >= col_ids, 0.0, -1e30).astype(jnp.float32)
    low_lane = lax.broadcasted_iota(jnp.int32, (half, LANES), 1) < head_width
    slot_ids = lax.broadcasted_iota(jnp.int32, (LANES, width_in), 0)
    head_ids = lax.broadcasted_iota(jnp.int32, (LANES, width_in), 1) // head_width
    pick_feed = jnp.where(slot_ids == head_ids + heads, 1.0, 0.0).astype(jnp.float32)
    pick_grow = jnp.where(slot_ids == head_ids + 2 * heads, 1.0, 0.0).astype(jnp.float32)

    cum_rows, cum_cols = [], []
    for b in range(blocks):
        span = slice(b * BLOCK, (b + 1) * BLOCK)
        cum_t = jnp.dot(
            decay_ref[:, span], upper, precision=EXACT, preferred_element_type=jnp.float32
        )
        feed_t = step_ref[:, span] * jnp.exp(cum_t[:, BLOCK - 1 : BLOCK] - cum_t)
        filler = jnp.zeros((LANES - 3 * heads, BLOCK), jnp.float32)
        cols = jnp.transpose(jnp.concatenate([cum_t, feed_t, jnp.exp(cum_t), filler], axis=0))
        cum_rows.append(cum_t)
        cum_cols.append(cols)
        feed = jnp.dot(cols, pick_feed, precision=EXACT, preferred_element_type=jnp.float32)
        spread[span, :] = jnp.dot(
            cols, pick_grow, precision=EXACT, preferred_element_type=jnp.float32
        )
        feed_rows = (signal_ref[span, :].astype(jnp.float32) * feed).astype(jnp.bfloat16)
        keys_t = jnp.transpose(keys_ref[span, :].astype(jnp.float32)).astype(jnp.bfloat16)
        local[b] = jnp.dot(keys_t, feed_rows, preferred_element_type=jnp.float32)

    def block_decay(b):
        last = (b + 1) * BLOCK - 1
        return spread[last : last + 1, :]

    def relay_copy(c):
        part = pl.ds(c * (state_width // RELAY_CHUNKS), state_width // RELAY_CHUNKS)
        return pltpu.make_async_remote_copy(
            src_ref=relay_out.at[part],
            dst_ref=relay_in.at[part],
            send_sem=relay_send.at[c],
            recv_sem=relay_recv.at[c],
            device_id={"seq": (seq + 1) % seq_count},
            device_id_type=MESH,
        )

    pl.semaphore_wait(barrier, count + 1)

    @pl.when(seq == 0)
    def _():
        relay_in[...] = jnp.zeros_like(relay_in)

    def relay():
        for c in range(RELAY_CHUNKS):
            n = state_width // RELAY_CHUNKS
            part = slice(c * n, (c + 1) * n)

            @pl.when(seq > 0)
            def _():
                relay_copy(c).wait_recv()

            @pl.when(seq < seq_count - 1)
            def _():
                state = relay_in[part, :].astype(jnp.float32)
                for b in range(blocks):
                    state = block_decay(b) * state + local[b, part, :]
                relay_out[part, :] = state.astype(jnp.bfloat16)
                relay_copy(c).start()

    def inner_pair(b, p, scores):
        cols = slice(p * LANES, (p + 1) * LANES)
        base = b * BLOCK
        signal_pair = signal_ref[base : base + BLOCK, cols]
        parts = []
        for top, wide in ((0, half), (half, BLOCK)):
            outs = []
            for h in (2 * p, 2 * p + 1):
                gaps = (
                    cum_cols[b][top : top + half, h : h + 1]
                    - cum_rows[b][h : h + 1, :wide]
                    + barred[top : top + half, :wide]
                )
                scaled = scores[top : top + half, :wide] * jnp.exp(gaps)
                scaled = scaled * step_ref[h : h + 1, base : base + wide]
                outs.append(
                    jnp.dot(
                        scaled.astype(jnp.bfloat16),
                        signal_pair[:wide],
                        preferred_element_type=jnp.float32,
                    )
                )
            parts.append(jnp.where(low_lane, outs[0], outs[1]))
        for number, value in enumerate(parts):
            at = slice(base + number * half, base + (number + 1) * half)
            inner[at, cols] = value + jnp.where(
                low_lane, skip_ref[2 * p], skip_ref[2 * p + 1]
            ) * signal_ref[at, cols].astype(jnp.float32)

    turn = 0
    pair_count = width_in // LANES
    every = max(1, blocks * pair_count // 3)
    done = 0
    for b in range(blocks):
        span = slice(b * BLOCK, (b + 1) * BLOCK)
        scores = lax.dot_general(
            query_ref[span, :],
            keys_ref[span, :],
            (((1,), (1,)), ((), ())),
            preferred_element_type=jnp.float32,
        )
        for p in range(pair_count):
            if done % every == 0 and turn < 3:
                pl.when(seq == turn)(relay)
                turn += 1
            inner_pair(b, p, scores)
            done += 1
    pl.when(seq >= turn)(relay)

    def multiply(t, dest, slot, part):
        @pl.loop(0, width // tile)
        def _(i):
            cols = pl.ds(pl.multiple_of(i * tile, tile), tile)
            dest[slot, part, cols] = jnp.dot(
                gained_ref[part, :], wbuf[t, :, cols], preferred_element_type=jnp.float32
            ).astype(jnp.bfloat16)

    def y_copy(s, c):
        part = pl.ds(c * rows, rows)
        return pltpu.make_async_remote_copy(
            src_ref=peer_out.at[s, part],
            dst_ref=peer_in.at[s, part],
            send_sem=y_send.at[s, c],
            recv_sem=y_recv.at[s, c],
            device_id={"mp": zm * PAIRS + 1 - ym},
            device_id_type=MESH,
        )

    sent = 0
    state = relay_in[...].astype(jnp.float32)
    for b in range(blocks):
        span = slice(b * BLOCK, (b + 1) * BLOCK)
        carried = state.astype(jnp.bfloat16)
        squared = jnp.zeros((BLOCK, LANES), jnp.float32)
        for p in range(pair_count):
            cols = slice(p * LANES, (p + 1) * LANES)
            read = jnp.dot(query_ref[span, :], carried[:, cols], preferred_element_type=jnp.float32)
            gate = gate_ref[span, cols].astype(jnp.float32)
            gated = (inner[span, cols] + spread[span, cols] * read) * (gate / (1.0 + jnp.exp(-gate)))
            squared = squared + gated * gated
            gained_ref[span, cols] = (gated * gain_ref[:, cols]).astype(jnp.bfloat16)
        square_sum[span, :] = squared
        if b == 0:
            w_copy(0).wait()
        multiply(0, peer_out, 0, span)
        while sent < CHUNKS and (sent + 1) * rows <= (b + 1) * BLOCK:
            y_copy(0, sent).start()
            sent += 1
        if b < blocks - 1:
            state = block_decay(b) * state + local[b]
    total_row = jnp.sum(jnp.transpose(square_sum[...]), axis=0, keepdims=True)
    squares_ref[...] = jnp.broadcast_to(total_row, (8, tokens))

    def sq_copy(d):
        return pltpu.make_async_remote_copy(
            src_ref=squares_ref,
            dst_ref=sq_in.at[me],
            send_sem=sq_send.at[d],
            recv_sem=sq_recv.at[me],
            device_id={"mp": (me + d) % count},
            device_id_type=MESH,
        )

    def sq_arrival(source):
        return pltpu.make_async_remote_copy(
            src_ref=squares_ref,
            dst_ref=sq_in.at[source],
            send_sem=sq_send.at[0],
            recv_sem=sq_recv.at[source],
            device_id={"mp": source},
            device_id_type=MESH,
        )

    def z_copy(s, c, way):
        part = pl.ds(c * rows, rows)
        dest, sems = (from_low, low_recv) if way > 0 else (from_high, high_recv)
        z = targets[s]
        return pltpu.make_async_remote_copy(
            src_ref=own.at[s, part],
            dst_ref=dest.at[z, part],
            send_sem=z_send.at[s, c],
            recv_sem=sems.at[z, c],
            device_id={"mp": (zm + way) * PAIRS + ym},
            device_id_type=MESH,
        )

    for d in range(1, count):
        sq_copy(d).start()

    def line_copy(s, e, way):
        dest = ((from_low, line_low), (from_high, line_high))[way < 0][e]
        sems = line_low_recv if way > 0 else line_high_recv
        z = targets[s]
        return pltpu.make_async_remote_copy(
            src_ref=(own, peer_out)[e].at[s, line_part],
            dst_ref=dest.at[z, line_part] if e == 0 else dest.at[z],
            send_sem=line_send.at[s, e],
            recv_sem=sems.at[z, e],
            device_id={"mp": (zm + way) * PAIRS + ym},
            device_id_type=MESH,
        )

    def line_arrival(s, e, way):
        dest = ((from_low, line_low), (from_high, line_high))[way < 0][e]
        sems = line_low_recv if way > 0 else line_high_recv
        z = targets[s]
        return pltpu.make_async_remote_copy(
            src_ref=(own, peer_out)[e].at[s, line_part],
            dst_ref=dest.at[z, line_part] if e == 0 else dest.at[z],
            send_sem=line_send.at[s, e],
            recv_sem=sems.at[z, e],
            device_id={"mp": (zm - way) * PAIRS + ym},
            device_id_type=MESH,
        )

    def cross_copy():
        return pltpu.make_async_remote_copy(
            src_ref=peer_out.at[lines - 1, line_part],
            dst_ref=peer_in.at[lines - 1, line_part],
            send_sem=cross_send.at[0],
            recv_sem=cross_recv.at[0],
            device_id={"mp": zm * PAIRS + 1 - ym},
            device_id_type=MESH,
        )

    def line_step(s):
        z = targets[s]
        for e in (1, 0):
            mine = (own, peer_out)[e]
            line_total[...] = mine[s, line_part, :].astype(jnp.float32)

            @pl.when(jnp.logical_and(z >= zm, zm > 0))
            def _():
                line_arrival(s, e, 1).wait_recv()
                came = from_low[z, line_part, :] if e == 0 else line_low[z]
                line_total[...] += came.astype(jnp.float32)

            @pl.when(jnp.logical_and(z <= zm, zm < lines - 1))
            def _():
                line_arrival(s, e, -1).wait_recv()
                came = from_high[z, line_part, :] if e == 0 else line_high[z]
                line_total[...] += came.astype(jnp.float32)

            if s < lines - 1:
                mine[s, line_part, :] = line_total[...].astype(jnp.bfloat16)

                @pl.when(z > zm)
                def _():
                    line_copy(s, e, 1).start()

                @pl.when(z < zm)
                def _():
                    line_copy(s, e, -1).start()
            elif e == 1:
                mine[s, line_part, :] = line_total[...].astype(jnp.bfloat16)
                cross_copy().start()

    def feed_step(s):
        everything = slice(0, tokens)
        if s > 0:
            w_copy(s).wait()
            multiply(s, peer_out, s, everything)
            for c in range(CHUNKS):
                y_copy(s, c).start()
        w_copy(lines + s).wait()
        multiply(lines + s, own, s, everything)
        line_step(s)

    feed_step(0)
    feed_step(1)

    squares = squares_ref[...]
    for d in range(1, count):
        source = (me + d) % count
        sq_arrival(source).wait_recv()
        squares = squares + sq_in[source]
    inverse = 1.0 / jnp.sqrt(squares[0:1] / (count * gained_ref.shape[1]) + 1e-05)
    scaling = jnp.transpose(jnp.broadcast_to(inverse, (128, tokens)))

    for s in range(lines):
        z = targets[s]
        if 0 < s < lines - 1:
            feed_step(s + 1)
        for c in range(CHUNKS):
            part = pl.ds(c * rows, rows)
            y_copy(s, c).wait_recv()
            total[...] = own[s, part, :].astype(jnp.float32) + peer_in[s, part, :].astype(
                jnp.float32
            )

            @pl.when(jnp.logical_and(z >= zm, zm > 0))
            def _():
                z_copy_in(z, c, from_low, low_recv, own, z_send, rows, zm - 1, ym).wait_recv()
                total[...] += from_low[z, part, :].astype(jnp.float32)

            @pl.when(jnp.logical_and(z <= zm, zm < lines - 1))
            def _():
                z_copy_in(z, c, from_high, high_recv, own, z_send, rows, zm + 1, ym).wait_recv()
                total[...] += from_high[z, part, :].astype(jnp.float32)

            if s < lines - 1:
                own[s, part, :] = total[...].astype(jnp.bfloat16)

                @pl.when(z > zm)
                def _():
                    z_copy(s, c, 1).start()

                @pl.when(z < zm)
                def _():
                    z_copy(s, c, -1).start()
            else:
                factor = scaling[c * rows : (c + 1) * rows]
                for k in range(width // 128):
                    cols = slice(k * 128, (k + 1) * 128)
                    out_ref[part, cols] = (total[:, cols] * factor).astype(jnp.bfloat16)

    cross_copy().wait_recv()
    line_total[...] += peer_in[lines - 1, line_part, :].astype(jnp.float32)
    factor = scaling[tokens - line_rows :]
    for k in range(width // 128):
        cols = slice(k * 128, (k + 1) * 128)
        out_ref[line_part, cols] = (line_total[:, cols] * factor).astype(jnp.bfloat16)

    cross_copy().wait_send()
    for s in range(lines - 1):
        z = targets[s]
        for e in (0, 1):

            @pl.when(z > zm)
            def _():
                line_copy(s, e, 1).wait_send()

            @pl.when(z < zm)
            def _():
                line_copy(s, e, -1).wait_send()

    @pl.when(seq < seq_count - 1)
    def _():
        for c in range(RELAY_CHUNKS):
            relay_copy(c).wait_send()

    for d in range(1, count):
        sq_copy(d).wait_send()
    for s in range(lines):
        z = targets[s]
        for c in range(CHUNKS):
            y_copy(s, c).wait_send()
            if s < lines - 1:

                @pl.when(z > zm)
                def _():
                    z_copy(s, c, 1).wait_send()

                @pl.when(z < zm)
                def _():
                    z_copy(s, c, -1).wait_send()


def z_copy_in(z, c, dest, sems, own, z_send, rows, near, ym):
    part = pl.ds(c * rows, rows)
    return pltpu.make_async_remote_copy(
        src_ref=own.at[0, part],
        dst_ref=dest.at[z, part],
        send_sem=z_send.at[0, c],
        recv_sem=sems.at[z, c],
        device_id={"mp": near * PAIRS + ym},
        device_id_type=MESH,
    )


def on_device(
    signal,
    gate_input,
    input_map,
    output_map,
    log_decay,
    step_size,
    skip_gain,
    norm_gain,
    out_weight,
):
    tokens, depth = signal.shape
    state_width = input_map.shape[1]
    count = lax.axis_size("mp")
    lines = count // PAIRS
    line_rows = tokens // LINE_SHARE
    width = out_weight.shape[1] // count
    dma = pltpu.SemaphoreType.DMA
    held = lambda n: pltpu.VMEM((n, tokens, width), jnp.bfloat16)
    whole = pl.BlockSpec(memory_space=pltpu.VMEM)
    return pl.pallas_call(
        layer_kernel,
        out_shape=jax.ShapeDtypeStruct((tokens, width), jnp.bfloat16),
        in_specs=[whole] * 6
        + [pl.BlockSpec(memory_space=pltpu.SMEM), whole]
        + [pl.BlockSpec(memory_space=pl.ANY)],
        out_specs=whole,
        scratch_shapes=[
            pltpu.VMEM((tokens, depth), jnp.bfloat16),
            pltpu.VMEM((8, tokens), jnp.float32),
            pltpu.VMEM((tokens, depth), jnp.float32),
            pltpu.VMEM((tokens // BLOCK, state_width, depth), jnp.float32),
            pltpu.VMEM((tokens, depth), jnp.float32),
            pltpu.VMEM((state_width, depth), jnp.bfloat16),
            pltpu.VMEM((state_width, depth), jnp.bfloat16),
            pltpu.VMEM((tokens, LANES), jnp.float32),
            pltpu.VMEM((line_rows, width), jnp.float32),
            pltpu.VMEM((lines, line_rows, width), jnp.bfloat16),
            pltpu.VMEM((lines, line_rows, width), jnp.bfloat16),
            pltpu.VMEM((2 * lines, depth, width), jnp.bfloat16),
            held(lines),
            held(lines),
            held(lines),
            held(lines),
            held(lines),
            pltpu.VMEM(((tokens - line_rows) // CHUNKS, width), jnp.float32),
            pltpu.VMEM((count, 8, tokens), jnp.float32),
            dma((2 * lines,)),
            dma((lines, CHUNKS)),
            dma((lines, CHUNKS)),
            dma((lines, CHUNKS)),
            dma((lines, CHUNKS)),
            dma((lines, CHUNKS)),
            dma((count,)),
            dma((count,)),
            dma((RELAY_CHUNKS,)),
            dma((RELAY_CHUNKS,)),
            dma((lines, 2)),
            dma((lines, 2)),
            dma((lines, 2)),
            dma((1,)),
            dma((1,)),
        ],
        compiler_params=pltpu.CompilerParams(
            collective_id=0, has_side_effects=True, vmem_limit_bytes=58 << 20
        ),
        name="layer",
    )(
        signal,
        gate_input,
        input_map,
        output_map,
        jnp.transpose(log_decay),
        jnp.transpose(step_size),
        skip_gain,
        norm_gain[None],
        out_weight,
    )


def solution(mesh):
    placed = (
        P("seq", "mp"),
        P("seq", "mp"),
        P("seq", None),
        P("seq", None),
        P("seq", "mp"),
        P("seq", "mp"),
        P("mp"),
        P("mp"),
        P("mp", None),
    )
    return jax.shard_map(
        on_device, mesh=mesh, in_specs=placed, out_specs=P("seq", "mp"), check_vma=False
    )
```
